256 devices in a mesh: ply: 2 (over x_hi), gx: 8 (over y, core), gy: 16 (over z, x_lo).
Axes of the slice: x: 4 (x_hi: 2, x_lo: 2; x = x_hi * 2 + x_lo), y: 4, z: 8, core: 2. Of those that a mesh axis runs over, the one named last changes fastest.
Arguments:
- coords: float32 [3, 2, 48, 96, 128], P(None, 'ply', 'gx', 'gy'), may hold values from 0 to 1
- strain: float32 [2, 48, 96, 128], P('ply', 'gx', 'gy'), may hold values from 0.1 to 10.1
- kappa_old: float32 [2, 48, 96, 128], P('ply', 'gx', 'gy'), may hold values from 1 to 3
- counts: int32 [2, 48, 96], P('ply', 'gx', 'gy'), may hold values from 0 to 128, as said below
- pair_mask: int32 [2, 48, 96, 26], P('ply', 'gx', 'gy'), may hold values from 0 to 1, as said below
Outputs:
- kappa_new: float32 [2, 48, 96, 128], P('ply', 'gx', 'gy')
- damage: float32 [2, 48, 96, 128], P('ply', 'gx', 'gy')
The draws below stay inside these ranges and needn't reach their ends.
Inputs may be any that keep to these rules, and one draw needn't show every extreme that they name: `counts`: blocks whose count is 0 form the plate's hole, the same through the thickness. pair_mask[a, k] equals pair_mask[a + o_k, 25 - k], o_k being the k-th offset, wherever both blocks lie in the grid.
All inputs are finite; a program needn't handle non-finite values.
Results may differ from the reference program's by a relative error of at most 0.0003.
Values sent between devices are 32-bit elements; how exact they have to be, the bound alone decides.
No kernel may reach another device: no remote copies, remote signals or barrier semaphores. Data moves between devices by JAX's collectives and lax.ppermute only.
A program may use at most 64 MiB of HBM per device.

```python
import math
import jax
import jax.numpy as jnp
from jax import lax

PTS = 128
NZ = 2
NX = 48
NY = 96


def make_offsets_drawn():
    listed = []
    for first in (-1, 0, 1):
        for second in (-1, 0, 1):
            for third in (-1, 0, 1):
                if (first, second, third) != (0, 0, 0):
                    listed.append((first, second, third))
    return listed


def draw_coords(key, part):
    side_key, depth_key = jax.random.split(jax.random.fold_in(key, 41))
    toward_high = jax.random.randint(side_key, (3, NZ, NX, NY, 1), 0, 2).astype(jnp.float32)
    spread = jax.random.uniform(depth_key, (3, NZ, NX, NY, PTS), jnp.float32, 0.0, 1.0)
    depth = spread * spread
    placed = toward_high * (1.0 - depth) + (1.0 - toward_high) * depth
    return placed.astype(jnp.float32)


def draw_strain(key, part):
    first_key = jax.random.fold_in(jax.random.fold_in(key, 11), 0)
    third_key = jax.random.fold_in(jax.random.fold_in(key, 11), 2)
    fourth_key = jax.random.fold_in(jax.random.fold_in(key, 11), 3)
    center = jax.random.uniform(third_key, (2,), jnp.float32, -0.9, 0.9)
    across = (2.0 * jnp.arange(NX, dtype=jnp.float32) + 1.0 - NX) / NX
    along = (2.0 * jnp.arange(NY, dtype=jnp.float32) + 1.0 - NY) / NY
    off_x = across[:, None] - center[0]
    off_y = along[None, :] - center[1]
    bump = 1.0 + 2.0 * jnp.exp(-(off_x * off_x + off_y * off_y) / 0.245)
    block_factor = jnp.exp(jax.random.uniform(fourth_key, (NZ, NX, NY, 1), jnp.float32, math.log(0.7), math.log(1.5)))
    base = jnp.exp(jax.random.uniform(first_key, (NZ, NX, NY, PTS), jnp.float32, math.log(0.3), math.log(1.5)))
    return (base * block_factor * bump[None, :, :, None]).astype(jnp.float32)


def draw_counts(key, part):
    across = jnp.arange(NX, dtype=jnp.int32)
    along = jnp.arange(NY, dtype=jnp.int32)
    scaled_x = (2 * across + 1 - NX) * 512 // NX
    scaled_y = (2 * along + 1 - NY) * 512 // NY
    inside = scaled_x[:, None] * scaled_x[:, None] + scaled_y[None, :] * scaled_y[None, :] < 28900
    filled = jax.random.randint(jax.random.fold_in(key, 23), (NZ, NX, NY), 16, 129)
    return jnp.where(inside[None], 0, filled).astype(jnp.int32)


def draw_pair_mask(key, part):
    near_offsets = make_offsets_drawn()
    halves = (jax.random.randint(jax.random.fold_in(key, 37), (NZ, NX, NY, 13), 0, 4) < 3).astype(jnp.int32)
    columns = [None] * 26
    for which in range(13):
        forward = near_offsets[13 + which]
        columns[13 + which] = halves[..., which]
        columns[12 - which] = jnp.roll(halves[..., which], forward, axis=(0, 1, 2))
    return jnp.stack(columns, -1).astype(jnp.int32)


def steps_of(rng, dims, cuts, smallest, largest):
    def one(dim, shards_of):
        draws = jax.random.uniform(jax.random.fold_in(jax.random.fold_in(rng, 6), dim), (shards_of,), jnp.float32, smallest / len(cuts), largest / len(cuts))
        return jnp.repeat(jnp.exp(draws), dims[dim] // shards_of).reshape((-1,) + (1,) * (len(dims) - dim - 1))

    level = one(*cuts[0])
    for cut in cuts[1:]:
        level = level * one(*cut)
    return level


def setup_inputs(seed: int = 0) -> dict:
    key_of = jax.random.split(jax.random.key(seed), 6)
    coords = draw_coords(jax.random.fold_in(key_of[5], 71), 0)
    strain = draw_strain(jax.random.fold_in(key_of[5], 71), 0)
    kappa_old = jnp.clip(jnp.exp(math.log(3.0) - 1.0986123 * jax.random.uniform(key_of[2], (NZ, NX, NY, PTS), jnp.float32) ** steps_of(key_of[2], (NZ, NX, NY, PTS), ((0, 2), (1, 8), (2, 16)), -0.2, 0.2)), 1.0, 3.0)
    counts = draw_counts(jax.random.fold_in(key_of[5], 71), 0)
    pair_mask = draw_pair_mask(jax.random.fold_in(key_of[5], 71), 0)
    return {"coords": coords, "strain": strain, "kappa_old": kappa_old, "counts": counts, "pair_mask": pair_mask}


def make_offsets():
    listed = []
    for first in (-1, 0, 1):
        for second in (-1, 0, 1):
            for third in (-1, 0, 1):
                listed.append((first, second, third))
    return listed


def bell_weights(center, beside, offset):
    squared = jnp.zeros((center.shape[1], center.shape[2], center.shape[2]), jnp.float32)
    for comp in range(3):
        gap = offset[comp] + beside[comp][:, None, :] - center[comp][:, :, None]
        squared = squared + gap * gap
    return jnp.square(jnp.maximum(0.0, 1.0 - squared))


def reference(coords, strain, kappa_old, counts, pair_mask):
    every_offset = make_offsets()
    slots = lax.broadcasted_iota(jnp.int32, strain.shape, 3)
    active = (slots < counts[..., None]).astype(jnp.float32)
    payload = jnp.concatenate([coords, (strain * active)[None], active[None]], 0)
    padded = jnp.pad(payload, ((0, 0), (1, 1), (1, 1), (1, 1), (0, 0)))

    def one_row(row_at):
        zero = row_at * 0
        layer_at = row_at // NX
        strip_at = row_at % NX
        window = lax.dynamic_slice(padded, (zero, layer_at, strip_at, zero, zero), (5, 3, 3, NY + 2, PTS))
        pair_flags = lax.dynamic_slice(pair_mask, (layer_at, strip_at, zero, zero), (1, 1, NY, 26))[0, 0].astype(jnp.float32)
        center = window[:, 1, 1, 1:NY + 1]
        totals = jnp.zeros((2, NY, PTS), jnp.float32)
        for which, offset in enumerate(every_offset):
            beside = window[:, 1 + offset[0], 1 + offset[1], 1 + offset[2]:1 + offset[2] + NY]
            weights = bell_weights(center, beside, offset)
            term = jnp.einsum('bij,cbj->cbi', weights, beside[3:5], precision=lax.Precision.HIGHEST)
            if offset != (0, 0, 0):
                flag_at = which if which < 13 else which - 1
                term = term * pair_flags[:, flag_at][None, :, None]
            totals = totals + term
        return totals

    totals = lax.map(one_row, jnp.arange(NZ * NX, dtype=jnp.int32))
    totals = totals.reshape(NZ, NX, 2, NY, PTS).transpose(2, 0, 1, 3, 4)
    weighted, weight_sum = totals[0], totals[1]
    averaged = active * weighted / (weight_sum + 1.0 - active)
    highest = jnp.max(averaged) + 1e-6
    kappa_new = jnp.maximum(kappa_old, 4.0 * averaged / highest)
    damage = active * (1.0 - jnp.exp(-(kappa_new - 1.0) / 2.5) / kappa_new)
    return kappa_new, damage
```

```python
import jax
import jax.numpy as jnp
from jax import lax
from jax.experimental import pallas as pl
from jax.experimental.pallas import tpu as pltpu
from jax.sharding import Mesh
from jax.sharding import PartitionSpec as P

BX = 6
BY = 6
PTS = 128
K = 32
WX = BX + 2
WY = BY + 2
AXES = ("ply", "y", "core", "z", "xlo")
F32 = jnp.float32
BF16 = jnp.bfloat16


def split2(v):
    high = v.astype(BF16).astype(F32)
    return high, (v - high).astype(BF16).astype(F32)


def split3(v):
    high, rest = v.astype(BF16).astype(F32), None
    rest = v - high
    mid = rest.astype(BF16).astype(F32)
    return high, mid, rest - mid


def window_kernel(
    shift_ref, flag_ref, own_ref, other_ref, xlo_ref, xhi_ref, ylo_ref, yhi_ref, avg_ref, top_ref, feat, cent, rows, bfeat, bcent, acc
):
    feat[...] = jnp.zeros_like(feat)
    cent[...] = jnp.zeros_like(cent)
    rows[...] = jnp.zeros_like(rows)
    shift = shift_ref[0]

    def emit(parts, strain, layer, x_at, y_at, base, stride, own_base):
        count = strain.shape[0]
        z_at = shift if layer else 0.0
        pos = (parts[0] + (z_at - 0.5), parts[1] + x_at, parts[2] + y_at)
        pieces = [split2(p) for p in pos]
        norm = jnp.zeros_like(strain)
        for high, low in pieces:
            p = high + low
            norm = norm + p * p
        highs = [p[0] for p in pieces]
        lows = [p[1] for p in pieces]
        one = jnp.ones_like(strain)
        listed = highs + lows + highs + lows + list(split3(1.0 - norm)) + [one] * 3
        for k, v in enumerate(listed):
            feat[pl.ds(base * K + k, count, stride=stride * K), :] = v
        live = jnp.where(strain > 0.0, 1.0, 0.0)
        for k, v in enumerate(list(split3(strain)) + [live]):
            rows[pl.ds(base * 8 + k, count, stride=stride * 8), :] = v
        if own_base is not None:
            highs = [2.0 * v for v in highs]
            lows = [2.0 * v for v in lows]
            listed = highs + highs + lows + lows + [one] * 3 + list(split3(-norm))
            for k, v in enumerate(listed):
                cent[pl.ds(own_base * K + k, count, stride=K), :] = v

    y_in = lax.broadcasted_iota(jnp.int32, (BY, PTS), 0).astype(F32) - (BY // 2)
    x_in = lax.broadcasted_iota(jnp.int32, (WX, PTS), 0).astype(F32) - (WX // 2)
    for layer, ref in enumerate((own_ref, other_ref)):
        for x in range(BX):
            emit(
                [ref[c, x] for c in range(3)], ref[3, x], layer, float(x - BX // 2), y_in,
                layer * WX * WY + (x + 1) * WY + 1, 1, x * BY if layer == 0 else None,
            )
        for ref2, x in ((xlo_ref, -1), (xhi_ref, BX)):
            emit(
                [ref2[layer * 4 + c] for c in range(3)], ref2[layer * 4 + 3], layer, float(x - BX // 2), y_in,
                layer * WX * WY + (x + 1) * WY + 1, 1, None,
            )
        for ref2, y in ((ylo_ref, -1), (yhi_ref, BY)):
            emit(
                [ref2[layer * 4 + c] for c in range(3)], ref2[layer * 4 + 3], layer, x_in, float(y - BY // 2),
                layer * WX * WY + y + 1, WY, None,
            )

    def to_bf16(b, carry):
        bfeat[b] = feat[pl.ds(pl.multiple_of(b * K, K), K), :].astype(BF16)
        return carry

    lax.fori_loop(0, 2 * WX * WY, to_bf16, 0, unroll=8)

    def turn(a, carry):
        bcent[a] = cent[pl.ds(pl.multiple_of(a * K, K), K), :].T.astype(BF16)
        return carry

    lax.fori_loop(0, BX * BY, turn, 0, unroll=4)

    window = [(layer, dx, dy) for layer in (0, 1) for dx in (0, 1, 2) for dy in (0, 1, 2)]

    def block(a, carry):
        base = (a // BY) * WY + a % BY
        center = bcent[a]
        total = jnp.zeros((8, PTS), F32)
        for t in range(0, 18, 2):
            at = [layer * WX * WY + dx * WY + dy + base for layer, dx, dy in window[t : t + 2]]
            rhs = jnp.concatenate([bfeat[b] for b in at], axis=1)
            gap = jnp.dot(center, rhs, preferred_element_type=F32)
            w = jnp.maximum(gap, 0.0)
            w = w * w
            high = w.astype(BF16)
            low = (w - high.astype(F32)).astype(BF16)
            lhs = jnp.concatenate(
                [rows[pl.ds(pl.multiple_of(b * 8, 8), 8), :] * flag_ref[a * 18 + t + n] for n, b in enumerate(at)], axis=1
            ).astype(BF16)
            for piece in (high, low):
                total = total + lax.dot_general(lhs, piece, (((1,), (1,)), ((), ())), preferred_element_type=F32)
        acc[pl.ds(pl.multiple_of(a * 8, 8), 8), :] = total
        return carry

    lax.fori_loop(0, BX * BY, block, 0)

    top = jnp.zeros((BY, PTS), F32)
    for x in range(BX):
        s = [acc[pl.ds(x * BY * 8 + k, BY, stride=8), :] for k in range(4)]
        live = jnp.where(own_ref[3, x] > 0.0, 1.0, 0.0)
        averaged = live * (s[0] + s[1] + s[2]) / (s[3] + 1.0 - live)
        avg_ref[x] = averaged
        top = jnp.maximum(top, averaged)
    top_ref[...] = jnp.max(top, axis=0, keepdims=True)


def window_sums(shift, flags, own, other, xlo, xhi, ylo, yhi, interpret=False):
    vm = pl.BlockSpec(memory_space=pltpu.VMEM)
    sm = pl.BlockSpec(memory_space=pltpu.SMEM)
    return pl.pallas_call(
        window_kernel,
        out_shape=(jax.ShapeDtypeStruct((BX, BY, PTS), F32), jax.ShapeDtypeStruct((1, PTS), F32)),
        in_specs=[sm, sm] + [vm] * 6,
        out_specs=(vm, vm),
        scratch_shapes=[
            pltpu.VMEM((2 * WX * WY * K, PTS), F32),
            pltpu.VMEM((BX * BY * K, PTS), F32),
            pltpu.VMEM((2 * WX * WY * 8, PTS), F32),
            pltpu.VMEM((2 * WX * WY, K, PTS), BF16),
            pltpu.VMEM((BX * BY, PTS, K), BF16),
            pltpu.VMEM((BX * BY * 8, PTS), F32),
        ],
        name="window_sums",
        interpret=interpret,
    )(shift, flags, own, other, xlo, xhi, ylo, yhi)


def on_device(coords, strain, kappa_old, counts, pair_mask):
    ply = lax.axis_index("ply")
    slots = lax.broadcasted_iota(jnp.int32, (BX, BY, PTS), 2)
    active = slots < counts[0][..., None]
    own = jnp.concatenate([coords[:, 0], jnp.where(active, strain[0], 0.0)[None]], 0)
    other = lax.ppermute(own, "ply", [(0, 1), (1, 0)])

    gx = ("y", "core")
    gy = ("z", "xlo")
    up = lambda n: [(i, i + 1) for i in range(n - 1)]
    down = lambda n: [(i + 1, i) for i in range(n - 1)]
    xlo = lax.ppermute(jnp.concatenate([own[:, BX - 1], other[:, BX - 1]], 0), gx, up(8))
    xhi = lax.ppermute(jnp.concatenate([own[:, 0], other[:, 0]], 0), gx, down(8))

    def column(y):
        inner = jnp.concatenate([own[:, :, y], other[:, :, y]], 0)
        return jnp.concatenate([xlo[:, y][:, None], inner, xhi[:, y][:, None]], 1)

    ylo = lax.ppermute(column(BY - 1), gy, up(16))
    yhi = lax.ppermute(column(0), gy, down(16))

    flags = pair_mask[0]
    flags = jnp.concatenate(
        [flags[..., 9:13], jnp.ones_like(flags[..., :1]), flags[..., 13:17], jnp.where(ply == 0, flags[..., 17:26], flags[..., 0:9])],
        -1,
    ).astype(F32)
    shift = (1.0 - 2.0 * ply.astype(F32)).reshape(1)
    averaged, top = window_sums(shift, flags.reshape(-1), own, other, xlo, xhi, ylo, yhi)

    spread = lax.all_to_all(
        jnp.broadcast_to(top, (128, PTS)), ("ply", "y", "z", "xlo"), 0, 0, tiled=True
    )
    top = jnp.max(spread, axis=0, keepdims=True)
    top = jnp.maximum(top, lax.ppermute(top, "core", [(0, 1), (1, 0)]))
    highest = jnp.max(top) + 1e-06
    kappa_new = jnp.maximum(kappa_old, 4.0 * averaged[None] / highest)
    damage = active[None].astype(F32) * (1.0 - jnp.exp(-(kappa_new - 1.0) / 2.5) / kappa_new)
    return (kappa_new, damage)


def solution(mesh):
    fine = Mesh(mesh.devices.reshape(2, 4, 2, 8, 2), AXES)
    gx, gy = ("y", "core"), ("z", "xlo")
    placed = (
        P(None, "ply", gx, gy, None),
        P("ply", gx, gy, None),
        P("ply", gx, gy, None),
        P("ply", gx, gy),
        P("ply", gx, gy, None),
    )
    return jax.shard_map(
        on_device,
        mesh=fine,
        in_specs=placed,
        out_specs=(P("ply", gx, gy, None), P("ply", gx, gy, None)),
        check_vma=False,
    )
```

```python
import functools

import jax
import jax.numpy as jnp
from jax import lax
from jax.experimental import pallas as pl
from jax.experimental.pallas import tpu as pltpu
from jax.sharding import Mesh
from jax.sharding import PartitionSpec as P

BX = 6
BY = 6
NB = BX * BY
WX = BX + 2
PTS = 128
K = 16
AXES = ("ply", "y", "core", "z", "xlo")
F32 = jnp.float32
BF16 = jnp.bfloat16
VMEM = pl.BlockSpec(memory_space=pltpu.VMEM)
SMEM = pl.BlockSpec(memory_space=pltpu.SMEM)


def pieces_of(v, count):
    out = []
    for n in range(count):
        high = v.astype(BF16).astype(F32)
        out.append(high)
        v = v - high
    return out


def positions(ref, row, count, stride, step, x_at, y_at, z_at):
    load = lambda c: ref[pl.ds(row + c * step, count, stride=stride), :]
    shifts = (z_at - 0.5, x_at, y_at)
    pieces = [pieces_of(load(c) + shifts[c], 2) for c in range(3)]
    norm = None
    for high, low in pieces:
        p = high + low
        norm = p * p if norm is None else norm + p * p
    return [p[0] for p in pieces], [p[1] for p in pieces], norm, load(3)


def put_neighbour(feat, rows, base, highs, lows, norm, strain):
    count = strain.shape[0]
    one = jnp.ones_like(strain)
    live = jnp.where(strain > 0.0, 1.0, -256.0)
    listed = highs + lows + highs + pieces_of(live - norm, 3) + [one] * 3 + [jnp.zeros_like(strain)]
    for k, v in enumerate(listed):
        feat[pl.ds(base * K + k, count, stride=K), :] = v
    rows[pl.ds(base, count), :] = strain


def put_center(cent, base, highs, lows, norm):
    count = norm.shape[0]
    one = jnp.ones_like(norm)
    twice = [2.0 * v for v in highs]
    listed = twice + twice + [2.0 * v for v in lows] + [one] * 3 + pieces_of(-norm, 3) + [jnp.zeros_like(norm)]
    for k, v in enumerate(listed):
        cent[pl.ds(base * K + k, count, stride=K), :] = v


def round_tiles(feat, bfeat, count, unroll):
    def one(b, carry):
        bfeat[b] = feat[pl.ds(pl.multiple_of(b * K, K), K), :].astype(BF16)
        return carry

    lax.fori_loop(0, count, one, 0, unroll=unroll)


def pair_sums(center, pairs, bfeat, rows, mask):
    spot = jnp.where(lax.broadcasted_iota(jnp.int32, (K, PTS), 0) == 9, 1.0, 0.0)
    sums = [[None] * 16, [None] * 16]
    for t in range(0, len(pairs), 2):
        some = pairs[t : t + 2]
        tiles = []
        for b, flag in some:
            tile = bfeat[b]
            if flag is not None:
                tile = tile + (spot * mask(*flag)).astype(BF16)
            tiles.append(tile)
        rhs = jnp.concatenate(tiles, axis=1) if len(tiles) > 1 else tiles[0]
        gap = jnp.dot(center, rhs, preferred_element_type=F32)
        for n, (b, flag) in enumerate(some):
            strain = jnp.broadcast_to(rows[pl.ds(b, 1), :], (8, PTS))
            for r in range(16):
                w = jnp.maximum(gap[r * 8 : r * 8 + 8, n * PTS : (n + 1) * PTS], 0.0)
                w = w * w
                v = w * strain
                sums[0][r] = v if sums[0][r] is None else sums[0][r] + v
                sums[1][r] = w if sums[1][r] is None else sums[1][r] + w
    return [jnp.sum(jnp.concatenate(s, axis=0).T, axis=0, keepdims=True) for s in sums]


def y_in():
    return lax.broadcasted_iota(jnp.int32, (BY, PTS), 0).astype(F32) - (BY // 2)


def mask_reader(mask_ref, place_ref):
    def read(a, layer, dx, dy):
        t = dx * 3 + dy
        if layer:
            k = jnp.where(place_ref[0] == 0, 17, 0) + t
        else:
            k = 9 + t - jnp.where(t > 4, 1, 0)
        return (mask_ref[a, 0, k] * 256 - 256).astype(F32)

    return read


def inner_sums(layer, bcent, bfeat, rows, mask, acc):
    def strip(x, first, dxs):
        for y in range(BY):
            a = x * BY + y
            pairs = []
            for n in range(dxs):
                for dy in range(3):
                    if 0 <= y + dy - 1 < BY:
                        flag = (a, layer, first + n - x + 1, dy)
                        if layer == 0 and dy == 1 and dxs == 3 and n == 1:
                            flag = None
                        pairs.append(((first + n) * BY + y + dy - 1, flag))
            for c, s in enumerate(pair_sums(bcent[a], pairs, bfeat, rows, mask)):
                acc[pl.ds(a * 2 + c, 1), :] = s

    def edge(e, carry):
        strip(e * (BX - 1), e * (BX - 2), 2)
        return carry

    def middle(x, carry):
        strip(x, x - 1, 3)
        return carry

    lax.fori_loop(0, 2, edge, 0)
    lax.fori_loop(1, BX - 1, middle, 0)


def own_kernel(place_ref, mask_ref, own_ref, acc, bcent, cent, feat, rows, bfeat):
    read = mask_reader(mask_ref, place_ref)

    def mask(a, layer, dx, dy):
        at_self = (dx == 1) if dy == 1 else False
        return read(a, layer, dx, dy) if dy != 1 else jnp.where(at_self, 0.0, read(a, layer, dx, dy))

    for x in range(BX):
        highs, lows, norm, strain = positions(own_ref, x * BY, BY, 1, NB, float(x - BX // 2), y_in(), 0.0)
        put_neighbour(feat, rows, x * BY, highs, lows, norm, strain)
        put_center(cent, x * BY, highs, lows, norm)
    round_tiles(feat, bfeat, NB, 6)

    def turn(a, carry):
        bcent[a] = cent[pl.ds(pl.multiple_of(a * K, K), K), :].T.astype(BF16)
        return carry

    lax.fori_loop(0, NB, turn, 0, unroll=6)
    inner_sums(0, bcent, bfeat, rows, mask, acc)


def other_kernel(place_ref, mask_ref, other_ref, bcent, acc, feat, rows, bfeat):
    shift = (1 - 2 * place_ref[0]).astype(F32)
    for x in range(BX):
        highs, lows, norm, strain = positions(other_ref, x * BY, BY, 1, NB, float(x - BX // 2), y_in(), shift)
        put_neighbour(feat, rows, x * BY, highs, lows, norm, strain)
    round_tiles(feat, bfeat, NB, 6)
    inner_sums(1, bcent, bfeat, rows, mask_reader(mask_ref, place_ref), acc)


def x_kernel(place_ref, mask_ref, core_ref, far_ref, bcent, acc, feat, rows, bfeat):
    shift = (1 - 2 * place_ref[0]).astype(F32)
    mask = mask_reader(mask_ref, place_ref)
    acc[...] = jnp.zeros_like(acc)
    for slot, ref in enumerate((core_ref, far_ref)):
        above = (1 - place_ref[1]) if slot == 0 else place_ref[1]
        x_at = (above * (BX + 1) - 1 - BX // 2).astype(F32)
        for layer in range(2):
            highs, lows, norm, strain = positions(ref, layer * 4 * BY, BY, 1, BY, x_at, y_in(), shift if layer else 0.0)
            put_neighbour(feat, rows, (slot * 2 + layer) * BY, highs, lows, norm, strain)
    round_tiles(feat, bfeat, 4 * BY, 6)

    def side(slot, carry):
        above = jnp.where(slot == 0, 1 - place_ref[1], place_ref[1])
        for y in range(BY):
            a = above * (BX - 1) * BY + y
            pairs = [
                ((slot * 2 + layer) * BY + y + dy - 1, (a, layer, above * 2, dy))
                for layer in range(2)
                for dy in range(3)
                if 0 <= y + dy - 1 < BY
            ]
            for c, s in enumerate(pair_sums(bcent[a], pairs, bfeat, rows, mask)):
                acc[pl.ds(a * 2 + c, 1), :] = s
        return carry

    lax.fori_loop(0, 2, side, 0)


def y_kernel(
    place_ref, mask_ref, near_ref, far_ref, bcent, own_ref, acc1, acc2, acc3, avg_ref, top_ref, feat, rows, bfeat, acc
):
    shift = (1 - 2 * place_ref[0]).astype(F32)
    mask = mask_reader(mask_ref, place_ref)
    acc[...] = acc1[...] + acc2[...] + acc3[...]
    x_in = lax.broadcasted_iota(jnp.int32, (WX, PTS), 0).astype(F32) - (WX // 2)
    for slot, ref in enumerate((near_ref, far_ref)):
        above = (1 - place_ref[2]) if slot == 0 else place_ref[2]
        y_at = (above * (BY + 1) - 1 - BY // 2).astype(F32)
        for layer in range(2):
            highs, lows, norm, strain = positions(ref, layer * 4 * WX, WX, 1, WX, x_in, y_at, shift if layer else 0.0)
            put_neighbour(feat, rows, (slot * 2 + layer) * WX, highs, lows, norm, strain)
    round_tiles(feat, bfeat, 4 * WX, 8)

    def side(slot, carry):
        above = jnp.where(slot == 0, 1 - place_ref[2], place_ref[2])
        for x in range(BX):
            a = above * (BY - 1) + x * BY
            pairs = [
                ((slot * 2 + layer) * WX + x + dx, (a, layer, dx, above * 2)) for layer in range(2) for dx in range(3)
            ]
            for c, s in enumerate(pair_sums(bcent[a], pairs, bfeat, rows, mask)):
                acc[pl.ds(a * 2 + c, 1), :] += s
        return carry

    lax.fori_loop(0, 2, side, 0)
    top = None
    for r in range(0, NB, 12):
        s = [acc[pl.ds(r * 2 + k, 12, stride=2), :] for k in range(2)]
        live = jnp.where(own_ref[pl.ds(3 * NB + r, 12), :] > 0.0, 1.0, 0.0)
        averaged = live * s[0] / (s[1] + 1.0 - live)
        avg_ref[pl.ds(r, 12), :] = averaged
        top = averaged if top is None else jnp.maximum(top, averaged)
    top_ref[...] = jnp.broadcast_to(jnp.max(top, axis=0, keepdims=True), (8, PTS))


def pack_kernel(counts_ref, coords_ref, strain_ref, own_ref):
    slots = lax.broadcasted_iota(jnp.int32, (1, PTS), 1)
    for c in range(3):
        own_ref[pl.ds(c * NB, NB), :] = coords_ref[pl.ds(c * NB, NB), 0, :]
    for b in range(NB):
        live = slots < counts_ref[b // BY, 0, b % BY]
        own_ref[pl.ds(3 * NB + b, 1), :] = jnp.where(live, strain_ref[b], 0.0)


def strips_kernel(place_ref, own_ref, other_ref, core_ref, far_ref):
    for slot, out in enumerate((core_ref, far_ref)):
        above = (1 - place_ref[1]) if slot == 0 else place_ref[1]
        for layer, ref in enumerate((own_ref, other_ref)):
            for c in range(4):
                out[pl.ds((layer * 4 + c) * BY, BY), :] = ref[pl.ds(c * NB + above * (BX - 1) * BY, BY), :]


def columns_kernel(place_ref, own_ref, other_ref, core_ref, far_ref, near_out, far_out):
    for slot, out in enumerate((near_out, far_out)):
        y = ((1 - place_ref[2]) if slot == 0 else place_ref[2]) * (BY - 1)
        for layer, ref in enumerate((own_ref, other_ref)):
            for c in range(4):
                row, halo = (layer * 4 + c) * WX, (layer * 4 + c) * BY
                out[pl.ds(row + 1, BX), :] = ref[pl.ds(c * NB + y, BX, stride=BY), :]
                out[pl.ds(row + (1 - place_ref[1]) * (WX - 1), 1), :] = core_ref[pl.ds(halo + y, 1), :]
                out[pl.ds(row + place_ref[1] * (WX - 1), 1), :] = far_ref[pl.ds(halo + y, 1), :]


def final_kernel(top_ref, avg_ref, old_ref, own_ref, new_ref, damage_ref):
    highest = jnp.max(top_ref[...], keepdims=True) + 1e-06
    for b in range(0, NB, 12):
        averaged = avg_ref[pl.ds(b, 12), :]
        live = jnp.where(own_ref[pl.ds(3 * NB + b, 12), :] > 0.0, 1.0, 0.0)
        new = jnp.maximum(old_ref[pl.ds(b, 12), 0, :], 4.0 * averaged / highest)
        new_ref[pl.ds(b, 12), 0, :] = new
        damage_ref[pl.ds(b, 12), 0, :] = live * (1.0 - jnp.exp(-(new - 1.0) / 2.5) / new)


def call(kernel, outs, in_specs, scratch=(), us=1):
    return pl.pallas_call(
        kernel,
        out_shape=tuple(jax.ShapeDtypeStruct(s, d) for s, d in outs),
        in_specs=in_specs,
        out_specs=tuple(VMEM for _ in outs),
        scratch_shapes=[pltpu.VMEM(s, d) for s, d in scratch],
        compiler_params=pltpu.CompilerParams(vmem_limit_bytes=16 << 20),
        cost_estimate=pl.CostEstimate(flops=us * 400_000_000, bytes_accessed=1 << 16, transcendentals=0),
        name=kernel.__name__,
    )


def feature_scratch(count):
    return [((count * K, PTS), F32), ((count, PTS), F32), ((count, K, PTS), BF16)]


SUMS = ((2 * NB, PTS), F32)


def on_device(coords, strain, kappa_old, counts, pair_mask):
    place = jnp.stack([lax.axis_index(a) for a in ("ply", "core", "xlo")]).astype(jnp.int32)
    mask = pair_mask.reshape(NB, 1, 26)
    (own,) = call(pack_kernel, [((4 * NB, PTS), F32)], [SMEM, VMEM, VMEM])(
        counts.reshape(BX, 1, BY), coords.reshape(3 * NB, 1, PTS), strain.reshape(NB, 1, PTS)
    )
    swap = [(0, 1), (1, 0)]
    beside = lambda n: [p for i in range(1, n - 1, 2) for p in ((i, i + 1), (i + 1, i))]
    other = lax.ppermute(own, "ply", swap)
    acc1, bcent = call(
        own_kernel, [SUMS, ((NB, PTS, K), BF16)], [SMEM, SMEM, VMEM], [((NB * K, PTS), F32)] + feature_scratch(NB), 5
    )(place, mask, own)

    strip = ((8 * BY, PTS), F32)
    core, far = call(strips_kernel, [strip, strip], [SMEM, VMEM, VMEM])(place, own, other)
    core = lax.ppermute(core, "core", swap)
    far = lax.ppermute(far, ("y", "core"), beside(8))
    (acc2,) = call(other_kernel, [SUMS], [SMEM, SMEM, VMEM, VMEM], feature_scratch(NB), 5)(place, mask, other, bcent)

    column = ((8 * WX, PTS), F32)
    ynear, yfar = call(columns_kernel, [column, column], [SMEM] + [VMEM] * 4)(place, own, other, core, far)
    ynear = lax.ppermute(ynear, "xlo", swap)
    yfar = lax.ppermute(yfar, ("z", "xlo"), beside(16))
    (acc3,) = call(x_kernel, [SUMS], [SMEM, SMEM] + [VMEM] * 3, feature_scratch(4 * BY), 2)(place, mask, core, far, bcent)
    averaged, top = call(
        y_kernel, [((NB, PTS), F32), ((8, PTS), F32)], [SMEM, SMEM] + [VMEM] * 7, feature_scratch(4 * WX) + [SUMS], 2
    )(place, mask, ynear, yfar, bcent, own, acc1, acc2, acc3)

    top = jnp.maximum(top, lax.ppermute(top, "core", swap))
    tops = lax.all_to_all(jnp.broadcast_to(top[:1], (128, PTS)), ("ply", "y", "z", "xlo"), 0, 0, tiled=True)
    new, damage = call(final_kernel, [((NB, 1, PTS), F32)] * 2, [VMEM] * 4)(tops, averaged, kappa_old.reshape(NB, 1, PTS), own)
    return (new.reshape(1, BX, BY, PTS), damage.reshape(1, BX, BY, PTS))


def solution(mesh):
    fine = Mesh(mesh.devices.reshape(2, 4, 2, 8, 2), AXES)
    gx, gy = ("y", "core"), ("z", "xlo")
    placed = (
        P(None, "ply", gx, gy, None),
        P("ply", gx, gy, None),
        P("ply", gx, gy, None),
        P("ply", gx, gy),
        P("ply", gx, gy, None),
    )
    return jax.shard_map(
        on_device,
        mesh=fine,
        in_specs=placed,
        out_specs=(P("ply", gx, gy, None), P("ply", gx, gy, None)),
        check_vma=False,
    )
```

```python
import jax
import jax.numpy as jnp
from jax import lax
from jax.experimental import pallas as pl
from jax.experimental.pallas import tpu as pltpu
from jax.sharding import Mesh
from jax.sharding import PartitionSpec as P

BX = 6
BY = 6
NB = BX * BY
WX = BX + 2
PTS = 128
K = 16
FLAGS = 32
AXES = ("ply", "y", "core", "z", "xlo")
F32 = jnp.float32
BF16 = jnp.bfloat16
VMEM = pl.BlockSpec(memory_space=pltpu.VMEM)


def pieces_of(v, count):
    out = []
    for n in range(count):
        high = v.astype(BF16).astype(F32)
        out.append(high)
        v = v - high
    return out


def positions(ref, row, count, stride, step, x_at, y_at, z_at):
    load = lambda c: ref[pl.ds(row + c * step, count, stride=stride), :]
    shifts = (z_at - 0.5, x_at, y_at)
    pieces = [pieces_of(load(c) + shifts[c], 2) for c in range(3)]
    norm = None
    for high, low in pieces:
        p = high + low
        norm = p * p if norm is None else norm + p * p
    return [p[0] for p in pieces], [p[1] for p in pieces], norm, load(3)


def put_neighbour(feat, rows, base, highs, lows, norm, strain):
    count = strain.shape[0]
    one = jnp.ones_like(strain)
    live = jnp.where(strain > 0.0, 1.0, -256.0)
    listed = highs + lows + highs + pieces_of(live - norm, 3) + [one] * 3 + [jnp.zeros_like(strain)]
    for k, v in enumerate(listed):
        feat[pl.ds(base * K + k, count, stride=K), :] = v
    rows[pl.ds(base, count), :] = strain


def put_center(cent, base, highs, lows, norm):
    count = norm.shape[0]
    one = jnp.ones_like(norm)
    twice = [2.0 * v for v in highs]
    listed = twice + twice + [2.0 * v for v in lows] + [one] * 3 + pieces_of(-norm, 3) + [jnp.zeros_like(norm)]
    for k, v in enumerate(listed):
        cent[pl.ds(base * K + k, count, stride=K), :] = v


def round_tiles(feat, bfeat, count, unroll):
    def one(b, carry):
        bfeat[b] = feat[pl.ds(pl.multiple_of(b * K, K), K), :].astype(BF16)
        return carry

    lax.fori_loop(0, count, one, 0, unroll=unroll)


def pair_sums(center, pairs, bfeat, rows, mask):
    spot = jnp.where(lax.broadcasted_iota(jnp.int32, (K, PTS), 0) == 9, 1.0, 0.0)
    sums = [[None] * 16, [None] * 16]
    for t in range(0, len(pairs), 2):
        some = pairs[t : t + 2]
        tiles = []
        for b, flag in some:
            tile = bfeat[b]
            if flag is not None:
                tile = tile + (spot * jnp.broadcast_to(mask[pl.ds(flag, 1), :], (K, PTS))).astype(BF16)
            tiles.append(tile)
        rhs = jnp.concatenate(tiles, axis=1) if len(tiles) > 1 else tiles[0]
        gap = jnp.dot(center, rhs, preferred_element_type=F32)
        for n, (b, flag) in enumerate(some):
            strain = jnp.broadcast_to(rows[pl.ds(b, 1), :], (8, PTS))
            for r in range(16):
                w = jnp.maximum(gap[r * 8 : r * 8 + 8, n * PTS : (n + 1) * PTS], 0.0)
                w = w * w
                v = w * strain
                sums[0][r] = v if sums[0][r] is None else sums[0][r] + v
                sums[1][r] = w if sums[1][r] is None else sums[1][r] + w
    return [jnp.sum(jnp.concatenate(s, axis=0).T, axis=0, keepdims=True) for s in sums]


def y_in():
    return lax.broadcasted_iota(jnp.int32, (BY, PTS), 0).astype(F32) - (BY // 2)


def flag_row(a, layer, dx, dy):
    t = dx * 3 + dy
    if layer:
        return a * FLAGS + t + jnp.where(lax.axis_index("ply") == 0, 17, 0)
    return a * FLAGS + jnp.where(t == 4, FLAGS - 1, 9 + t - jnp.where(t > 4, 1, 0))


def fill_flags(mask_ref, turned, flags):
    turned[...] = jnp.zeros_like(turned)
    turned[0:NB, 0:26] = (mask_ref[:, 0, :] * 256 - 256).astype(F32)
    across = turned[...].T
    for a in range(NB):
        flags[a * FLAGS : (a + 1) * FLAGS, :] = jnp.broadcast_to(across[0:FLAGS, a : a + 1], (FLAGS, PTS))


def strip_sums(layer, x, first, dxs, bcent, bfeat, rows, flags, acc, add):
    for y in range(BY):
        a = x * BY + y
        pairs = []
        for n in range(dxs):
            for dy in range(3):
                if 0 <= y + dy - 1 < BY:
                    at_self = layer == 0 and dy == 1 and dxs == 3 and n == 1
                    flag = None if at_self else flag_row(a, layer, first + n - x + 1, dy)
                    pairs.append(((first + n) * BY + y + dy - 1, flag))
        for c, s in enumerate(pair_sums(bcent[a], pairs, bfeat, rows, flags)):
            if add:
                s = s + acc[pl.ds(a * 2 + c, 1), :]
            acc[pl.ds(a * 2 + c, 1), :] = s


def edges(layer, add, *refs):
    def edge(e, carry):
        strip_sums(layer, e * (BX - 1), e * (BX - 2), 2, *refs, add)
        return carry

    lax.fori_loop(0, 2, edge, 0)


def middles(layer, low, high, add, *refs):
    def middle(x, carry):
        strip_sums(layer, x, x - 1, 3, *refs, add)
        return carry

    lax.fori_loop(low, high, middle, 0)


def other_shift():
    return (1 - 2 * lax.axis_index("ply")).astype(F32)


def own_kernel(mask_ref, own_ref, acc, bcent, flags, turned, cent, feat, rows, bfeat):
    fill_flags(mask_ref, turned, flags)
    for x in range(BX):
        highs, lows, norm, strain = positions(own_ref, x * BY, BY, 1, NB, float(x - BX // 2), y_in(), 0.0)
        put_neighbour(feat, rows, x * BY, highs, lows, norm, strain)
        put_center(cent, x * BY, highs, lows, norm)
    round_tiles(feat, bfeat, NB, 6)

    def turn(a, carry):
        bcent[a] = cent[pl.ds(pl.multiple_of(a * K, K), K), :].T.astype(BF16)
        return carry

    lax.fori_loop(0, NB, turn, 0, unroll=6)
    refs = (bcent, bfeat, rows, flags, acc)
    edges(0, False, *refs)
    middles(0, 1, BX - 1, False, *refs)


def other_kernel(other_ref, bcent, flags, before, acc, rows, bfeat, feat):
    for x in range(BX):
        highs, lows, norm, strain = positions(other_ref, x * BY, BY, 1, NB, float(x - BX // 2), y_in(), other_shift())
        put_neighbour(feat, rows, x * BY, highs, lows, norm, strain)
    round_tiles(feat, bfeat, NB, 6)
    acc[...] = before[...]
    refs = (bcent, bfeat, rows, flags, acc)
    edges(1, True, *refs)
    middles(1, 1, 2, True, *refs)


def x_kernel(core_ref, far_ref, bcent, flags, other_rows, other_bfeat, before, acc, feat, rows, bfeat):
    core = lax.axis_index("core")
    for slot, ref in enumerate((core_ref, far_ref)):
        above = (1 - core) if slot == 0 else core
        x_at = (above * (BX + 1) - 1 - BX // 2).astype(F32)
        for layer in range(2):
            highs, lows, norm, strain = positions(
                ref, layer * 4 * BY, BY, 1, BY, x_at, y_in(), other_shift() if layer else 0.0
            )
            put_neighbour(feat, rows, (slot * 2 + layer) * BY, highs, lows, norm, strain)
    round_tiles(feat, bfeat, 4 * BY, 6)
    acc[...] = before[...]

    def side(slot, carry):
        above = jnp.where(slot == 0, 1 - core, core)
        for y in range(BY):
            a = above * (BX - 1) * BY + y
            pairs = [
                ((slot * 2 + layer) * BY + y + dy - 1, flag_row(a, layer, above * 2, dy))
                for layer in range(2)
                for dy in range(3)
                if 0 <= y + dy - 1 < BY
            ]
            for c, s in enumerate(pair_sums(bcent[a], pairs, bfeat, rows, flags)):
                acc[pl.ds(a * 2 + c, 1), :] += s
        return carry

    lax.fori_loop(0, 2, side, 0)
    middles(1, 2, BX - 1, True, bcent, other_bfeat, other_rows, flags, acc)


def y_kernel(near_ref, far_ref, bcent, flags, own_ref, before, avg_ref, top_ref, feat, rows, bfeat, acc):
    xlo = lax.axis_index("xlo")
    acc[...] = before[...]
    x_in = lax.broadcasted_iota(jnp.int32, (WX, PTS), 0).astype(F32) - (WX // 2)
    for slot, ref in enumerate((near_ref, far_ref)):
        above = (1 - xlo) if slot == 0 else xlo
        y_at = (above * (BY + 1) - 1 - BY // 2).astype(F32)
        for layer in range(2):
            highs, lows, norm, strain = positions(
                ref, layer * 4 * WX, WX, 1, WX, x_in, y_at, other_shift() if layer else 0.0
            )
            put_neighbour(feat, rows, (slot * 2 + layer) * WX, highs, lows, norm, strain)
    round_tiles(feat, bfeat, 4 * WX, 8)

    def side(slot, carry):
        above = jnp.where(slot == 0, 1 - xlo, xlo)
        for x in range(BX):
            a = above * (BY - 1) + x * BY
            pairs = [
                ((slot * 2 + layer) * WX + x + dx, flag_row(a, layer, dx, above * 2))
                for layer in range(2)
                for dx in range(3)
            ]
            for c, s in enumerate(pair_sums(bcent[a], pairs, bfeat, rows, flags)):
                acc[pl.ds(a * 2 + c, 1), :] += s
        return carry

    lax.fori_loop(0, 2, side, 0)
    top = None
    for r in range(0, NB, 12):
        s = [acc[pl.ds(r * 2 + k, 12, stride=2), :] for k in range(2)]
        live = jnp.where(own_ref[pl.ds(3 * NB + r, 12), :] > 0.0, 1.0, 0.0)
        averaged = live * s[0] / (s[1] + 1.0 - live)
        avg_ref[pl.ds(r, 12), :] = averaged
        top = averaged if top is None else jnp.maximum(top, averaged)
    top_ref[...] = jnp.broadcast_to(jnp.max(top, axis=0, keepdims=True), (8, PTS))


def pack_kernel(counts_hbm, coords_hbm, strain_hbm, own_ref, counts_ref, coords_ref, strain_ref, sems):
    copies = [
        pltpu.make_async_copy(source, target, sems.at[n])
        for n, (source, target) in enumerate(
            ((counts_hbm, counts_ref), (strain_hbm, strain_ref), (coords_hbm, coords_ref))
        )
    ]
    for copy in copies:
        copy.start()
    for copy in copies:
        copy.wait()
    slots = lax.broadcasted_iota(jnp.int32, (1, PTS), 1)
    for c in range(3):
        own_ref[pl.ds(c * NB, NB), :] = coords_ref[pl.ds(c * NB, NB), 0, :]
    for b in range(NB):
        live = slots < counts_ref[b // BY, 0, b % BY]
        own_ref[pl.ds(3 * NB + b, 1), :] = jnp.where(live, strain_ref[b], 0.0)


def strips_kernel(own_ref, other_ref, core_ref, far_ref):
    core = lax.axis_index("core")
    for slot, out in enumerate((core_ref, far_ref)):
        above = (1 - core) if slot == 0 else core
        for layer, ref in enumerate((own_ref, other_ref)):
            for c in range(4):
                out[pl.ds((layer * 4 + c) * BY, BY), :] = ref[pl.ds(c * NB + above * (BX - 1) * BY, BY), :]


def columns_kernel(own_ref, other_ref, core_ref, far_ref, near_out, far_out):
    core, xlo = lax.axis_index("core"), lax.axis_index("xlo")
    for slot, out in enumerate((near_out, far_out)):
        y = ((1 - xlo) if slot == 0 else xlo) * (BY - 1)
        for layer, ref in enumerate((own_ref, other_ref)):
            for c in range(4):
                row, halo = (layer * 4 + c) * WX, (layer * 4 + c) * BY
                out[pl.ds(row + 1, BX), :] = ref[pl.ds(c * NB + y, BX, stride=BY), :]
                out[pl.ds(row + (1 - core) * (WX - 1), 1), :] = core_ref[pl.ds(halo + y, 1), :]
                out[pl.ds(row + core * (WX - 1), 1), :] = far_ref[pl.ds(halo + y, 1), :]


def final_kernel(top_ref, avg_ref, old_ref, own_ref, new_ref, damage_ref):
    highest = jnp.max(top_ref[...], keepdims=True) + 1e-06
    for b in range(0, NB, 12):
        averaged = avg_ref[pl.ds(b, 12), :]
        live = jnp.where(own_ref[pl.ds(3 * NB + b, 12), :] > 0.0, 1.0, 0.0)
        new = jnp.maximum(old_ref[pl.ds(b, 12), 0, :], 4.0 * averaged / highest)
        new_ref[pl.ds(b, 12), 0, :] = new
        damage_ref[pl.ds(b, 12), 0, :] = live * (1.0 - jnp.exp(-(new - 1.0) / 2.5) / new)


def call(kernel, outs, ins, scratch=(), us=1, space=VMEM, extra=()):
    return pl.pallas_call(
        kernel,
        out_shape=tuple(jax.ShapeDtypeStruct(s, d) for s, d in outs),
        in_specs=[space] * ins,
        out_specs=tuple(VMEM for _ in outs),
        scratch_shapes=[pltpu.VMEM(s, d) for s, d in scratch] + list(extra),
        compiler_params=pltpu.CompilerParams(vmem_limit_bytes=16 << 20),
        cost_estimate=pl.CostEstimate(flops=us * 400_000_000, bytes_accessed=1 << 16, transcendentals=0),
        name=kernel.__name__,
    )


def feature_scratch(count):
    return [((count * K, PTS), F32), ((count, PTS), F32), ((count, K, PTS), BF16)]


SUMS = ((2 * NB, PTS), F32)


def on_device(coords, strain, kappa_old, counts, pair_mask):
    (own,) = call(
        pack_kernel,
        [((4 * NB, PTS), F32)],
        3,
        space=pl.BlockSpec(memory_space=pltpu.HBM),
        extra=[
            pltpu.SMEM((BX, 1, BY), jnp.int32),
            pltpu.VMEM((3 * NB, 1, PTS), F32),
            pltpu.VMEM((NB, 1, PTS), F32),
            pltpu.SemaphoreType.DMA((3,)),
        ],
    )(counts.reshape(BX, 1, BY), coords.reshape(3 * NB, 1, PTS), strain.reshape(NB, 1, PTS))
    swap = [(0, 1), (1, 0)]
    beside = lambda n: [p for i in range(1, n - 1, 2) for p in ((i, i + 1), (i + 1, i))]
    other = lax.ppermute(own, "ply", swap)
    acc, bcent, flags = call(
        own_kernel,
        [SUMS, ((NB, PTS, K), BF16), ((NB * FLAGS, PTS), F32)],
        2,
        [((PTS, PTS), F32), ((NB * K, PTS), F32)] + feature_scratch(NB),
        6,
    )(pair_mask.reshape(NB, 1, 26), own)

    strip = ((8 * BY, PTS), F32)
    core, far = call(strips_kernel, [strip, strip], 2)(own, other)
    core = lax.ppermute(core, "core", swap)
    far = lax.ppermute(far, ("y", "core"), beside(8))
    tile = feature_scratch(NB)
    acc, rows, bfeat = call(other_kernel, [SUMS] + tile[1:], 4, tile[:1], 3)(other, bcent, flags, acc)

    column = ((8 * WX, PTS), F32)
    ynear, yfar = call(columns_kernel, [column, column], 4)(own, other, core, far)
    ynear = lax.ppermute(ynear, "xlo", swap)
    yfar = lax.ppermute(yfar, ("z", "xlo"), beside(16))
    (acc,) = call(x_kernel, [SUMS], 7, feature_scratch(4 * BY), 4)(core, far, bcent, flags, rows, bfeat, acc)
    averaged, top = call(y_kernel, [((NB, PTS), F32), ((8, PTS), F32)], 6, feature_scratch(4 * WX) + [SUMS], 2)(
        ynear, yfar, bcent, flags, own, acc
    )

    top = jnp.maximum(top, lax.ppermute(top, "core", swap))
    tops = lax.all_to_all(jnp.broadcast_to(top[:1], (128, PTS)), ("ply", "y", "z", "xlo"), 0, 0, tiled=True)
    new, damage = call(final_kernel, [((NB, 1, PTS), F32)] * 2, 4)(tops, averaged, kappa_old.reshape(NB, 1, PTS), own)
    return (new.reshape(1, BX, BY, PTS), damage.reshape(1, BX, BY, PTS))


def solution(mesh):
    fine = Mesh(mesh.devices.reshape(2, 4, 2, 8, 2), AXES)
    gx, gy = ("y", "core"), ("z", "xlo")
    placed = (
        P(None, "ply", gx, gy, None),
        P("ply", gx, gy, None),
        P("ply", gx, gy, None),
        P("ply", gx, gy),
        P("ply", gx, gy, None),
    )
    return jax.shard_map(
        on_device,
        mesh=fine,
        in_specs=placed,
        out_specs=(P("ply", gx, gy, None), P("ply", gx, gy, None)),
        check_vma=False,
    )
```

```python
import jax
import jax.numpy as jnp
from jax import lax
from jax.experimental import pallas as pl
from jax.experimental.pallas import tpu as pltpu
from jax.sharding import Mesh
from jax.sharding import PartitionSpec as P

BX = 6
BY = 6
NB = BX * BY
WX = BX + 2
PTS = 128
K = 16
FLAGS = 32
AXES = ("ply", "y", "core", "z", "xlo")
F32 = jnp.float32
BF16 = jnp.bfloat16
VMEM = pl.BlockSpec(memory_space=pltpu.VMEM)


def pieces_of(v, count):
    out = []
    for n in range(count):
        high = v.astype(BF16).astype(F32)
        out.append(high)
        v = v - high
    return out


def positions(ref, row, count, stride, step, x_at, y_at, z_at):
    load = lambda c: ref[pl.ds(row + c * step, count, stride=stride), :]
    shifts = (z_at - 0.5, x_at, y_at)
    pieces = [pieces_of(load(c) + shifts[c], 2) for c in range(3)]
    norm = None
    for high, low in pieces:
        p = high + low
        norm = p * p if norm is None else norm + p * p
    return [p[0] for p in pieces], [p[1] for p in pieces], norm, load(3)


def put_neighbour(feat, rows, base, highs, lows, norm, strain):
    count = strain.shape[0]
    one = jnp.ones_like(strain)
    live = jnp.where(strain > 0.0, 1.0, -256.0)
    listed = highs + lows + highs + pieces_of(live - norm, 3) + [one] * 3 + [jnp.zeros_like(strain)]
    for k, v in enumerate(listed):
        feat[pl.ds(base * K + k, count, stride=K), :] = v
    rows[pl.ds(base, count), :] = strain


def put_center(cent, base, highs, lows, norm):
    count = norm.shape[0]
    one = jnp.ones_like(norm)
    twice = [2.0 * v for v in highs]
    listed = twice + twice + [2.0 * v for v in lows] + [one] * 3 + pieces_of(-norm, 3) + [jnp.zeros_like(norm)]
    for k, v in enumerate(listed):
        cent[pl.ds(base * K + k, count, stride=K), :] = v


def round_tiles(feat, bfeat, count, unroll):
    def one(b, carry):
        bfeat[b] = feat[pl.ds(pl.multiple_of(b * K, K), K), :].astype(BF16)
        return carry

    lax.fori_loop(0, count, one, 0, unroll=unroll)


def pair_sums(center, pairs, bfeat, rows, mask):
    spot = jnp.where(lax.broadcasted_iota(jnp.int32, (K, PTS), 0) == 9, 1.0, 0.0)
    sums = [[None] * 16, [None] * 16]
    for t in range(0, len(pairs), 2):
        some = pairs[t : t + 2]
        tiles = []
        for b, flag in some:
            tile = bfeat[b]
            if flag is not None:
                tile = tile + (spot * jnp.broadcast_to(mask[pl.ds(flag, 1), :], (K, PTS))).astype(BF16)
            tiles.append(tile)
        rhs = jnp.concatenate(tiles, axis=1) if len(tiles) > 1 else tiles[0]
        gap = jnp.dot(center, rhs, preferred_element_type=F32)
        for n, (b, flag) in enumerate(some):
            strain = jnp.broadcast_to(rows[pl.ds(b, 1), :], (8, PTS))
            for r in range(16):
                w = jnp.maximum(gap[r * 8 : r * 8 + 8, n * PTS : (n + 1) * PTS], 0.0)
                w = w * w
                v = w * strain
                sums[0][r] = v if sums[0][r] is None else sums[0][r] + v
                sums[1][r] = w if sums[1][r] is None else sums[1][r] + w
    return [jnp.sum(jnp.concatenate(s, axis=0).T, axis=0, keepdims=True) for s in sums]


def y_in():
    return lax.broadcasted_iota(jnp.int32, (BY, PTS), 0).astype(F32) - (BY // 2)


def flag_row(a, layer, dx, dy):
    t = dx * 3 + dy
    if layer:
        return a * FLAGS + t + jnp.where(lax.axis_index("ply") == 0, 17, 0)
    return a * FLAGS + jnp.where(t == 4, FLAGS - 1, 9 + t - jnp.where(t > 4, 1, 0))


def fill_flags(mask_ref, turned, flags):
    turned[...] = jnp.zeros_like(turned)
    turned[0:NB, 0:26] = (mask_ref[:, 0, :] * 256 - 256).astype(F32)
    across = turned[...].T
    for a in range(NB):
        flags[a * FLAGS : (a + 1) * FLAGS, :] = jnp.broadcast_to(across[0:FLAGS, a : a + 1], (FLAGS, PTS))


def strip_sums(layer, x, first, dxs, bcent, bfeat, rows, flags, acc, add):
    for y in range(BY):
        a = x * BY + y
        pairs = []
        for n in range(dxs):
            for dy in range(3):
                if 0 <= y + dy - 1 < BY:
                    at_self = layer == 0 and dy == 1 and dxs == 3 and n == 1
                    flag = None if at_self else flag_row(a, layer, first + n - x + 1, dy)
                    pairs.append(((first + n) * BY + y + dy - 1, flag))
        for c, s in enumerate(pair_sums(bcent[a], pairs, bfeat, rows, flags)):
            if add:
                s = s + acc[pl.ds(a * 2 + c, 1), :]
            acc[pl.ds(a * 2 + c, 1), :] = s


def edges(layer, add, *refs):
    def edge(e, carry):
        strip_sums(layer, e * (BX - 1), e * (BX - 2), 2, *refs, add)
        return carry

    lax.fori_loop(0, 2, edge, 0, unroll=2)


def middles(layer, low, high, add, unroll, *refs):
    def middle(x, carry):
        strip_sums(layer, x, x - 1, 3, *refs, add)
        return carry

    lax.fori_loop(low, high, middle, 0, unroll=unroll)


def other_shift():
    return (1 - 2 * lax.axis_index("ply")).astype(F32)


def own_kernel(mask_ref, own_ref, acc, bcent, flags, rows, bfeat, turned, cent, feat):
    fill_flags(mask_ref, turned, flags)
    for x in range(BX):
        highs, lows, norm, strain = positions(own_ref, x * BY, BY, 1, NB, float(x - BX // 2), y_in(), 0.0)
        put_neighbour(feat, rows, x * BY, highs, lows, norm, strain)
        put_center(cent, x * BY, highs, lows, norm)
    round_tiles(feat, bfeat, NB, 6)

    def turn(a, carry):
        bcent[a] = cent[pl.ds(pl.multiple_of(a * K, K), K), :].T.astype(BF16)
        return carry

    lax.fori_loop(0, NB, turn, 0, unroll=6)
    refs = (bcent, bfeat, rows, flags, acc)
    edges(0, False, *refs)
    middles(0, 1, BX - 2, False, 3, *refs)
    acc[pl.ds(2 * (BX - 2) * BY, 2 * BY), :] = jnp.zeros((2 * BY, PTS), F32)


def other_kernel(other_ref, bcent, flags, before, acc, rows, bfeat, feat):
    for x in range(BX):
        highs, lows, norm, strain = positions(other_ref, x * BY, BY, 1, NB, float(x - BX // 2), y_in(), other_shift())
        put_neighbour(feat, rows, x * BY, highs, lows, norm, strain)
    round_tiles(feat, bfeat, NB, 6)
    acc[...] = before[...]
    refs = (bcent, bfeat, rows, flags, acc)
    edges(1, True, *refs)
    middles(1, 1, 2, True, 1, *refs)


def x_kernel(
    core_ref, far_ref, bcent, flags, own_rows, own_bfeat, other_rows, other_bfeat, before, acc, feat, rows, bfeat
):
    core = lax.axis_index("core")
    for slot, ref in enumerate((core_ref, far_ref)):
        above = (1 - core) if slot == 0 else core
        x_at = (above * (BX + 1) - 1 - BX // 2).astype(F32)
        for layer in range(2):
            highs, lows, norm, strain = positions(
                ref, layer * 4 * BY, BY, 1, BY, x_at, y_in(), other_shift() if layer else 0.0
            )
            put_neighbour(feat, rows, (slot * 2 + layer) * BY, highs, lows, norm, strain)
    round_tiles(feat, bfeat, 4 * BY, 6)
    acc[...] = before[...]

    def side(slot, carry):
        above = jnp.where(slot == 0, 1 - core, core)
        for y in range(BY):
            a = above * (BX - 1) * BY + y
            pairs = [
                ((slot * 2 + layer) * BY + y + dy - 1, flag_row(a, layer, above * 2, dy))
                for layer in range(2)
                for dy in range(3)
                if 0 <= y + dy - 1 < BY
            ]
            for c, s in enumerate(pair_sums(bcent[a], pairs, bfeat, rows, flags)):
                acc[pl.ds(a * 2 + c, 1), :] += s
        return carry

    lax.fori_loop(0, 2, side, 0, unroll=2)
    middles(0, BX - 2, BX - 1, True, 1, bcent, own_bfeat, own_rows, flags, acc)
    middles(1, 2, BX - 1, True, 3, bcent, other_bfeat, other_rows, flags, acc)


def y_kernel(near_ref, far_ref, bcent, flags, own_ref, before, avg_ref, top_ref, feat, rows, bfeat, acc):
    xlo = lax.axis_index("xlo")
    acc[...] = before[...]
    x_in = lax.broadcasted_iota(jnp.int32, (WX, PTS), 0).astype(F32) - (WX // 2)
    for slot, ref in enumerate((near_ref, far_ref)):
        above = (1 - xlo) if slot == 0 else xlo
        y_at = (above * (BY + 1) - 1 - BY // 2).astype(F32)
        for layer in range(2):
            highs, lows, norm, strain = positions(
                ref, layer * 4 * WX, WX, 1, WX, x_in, y_at, other_shift() if layer else 0.0
            )
            put_neighbour(feat, rows, (slot * 2 + layer) * WX, highs, lows, norm, strain)
    round_tiles(feat, bfeat, 4 * WX, 8)

    def side(slot, carry):
        above = jnp.where(slot == 0, 1 - xlo, xlo)
        for x in range(BX):
            a = above * (BY - 1) + x * BY
            pairs = [
                ((slot * 2 + layer) * WX + x + dx, flag_row(a, layer, dx, above * 2))
                for layer in range(2)
                for dx in range(3)
            ]
            for c, s in enumerate(pair_sums(bcent[a], pairs, bfeat, rows, flags)):
                acc[pl.ds(a * 2 + c, 1), :] += s
        return carry

    lax.fori_loop(0, 2, side, 0, unroll=2)
    top = None
    for r in range(0, NB, 12):
        s = [acc[pl.ds(r * 2 + k, 12, stride=2), :] for k in range(2)]
        live = jnp.where(own_ref[pl.ds(3 * NB + r, 12), :] > 0.0, 1.0, 0.0)
        averaged = live * s[0] / (s[1] + 1.0 - live)
        avg_ref[pl.ds(r, 12), :] = averaged
        top = averaged if top is None else jnp.maximum(top, averaged)
    top_ref[...] = jnp.broadcast_to(jnp.max(top, axis=0, keepdims=True), (8, PTS))


def pack_kernel(counts_hbm, coords_hbm, strain_hbm, own_ref, counts_ref, coords_ref, strain_ref, sems):
    copies = [
        pltpu.make_async_copy(source, target, sems.at[n])
        for n, (source, target) in enumerate(
            ((counts_hbm, counts_ref), (strain_hbm, strain_ref), (coords_hbm, coords_ref))
        )
    ]
    for copy in copies:
        copy.start()
    for copy in copies:
        copy.wait()
    slots = lax.broadcasted_iota(jnp.int32, (1, PTS), 1)
    for c in range(3):
        own_ref[pl.ds(c * NB, NB), :] = coords_ref[pl.ds(c * NB, NB), 0, :]
    for b in range(NB):
        live = slots < counts_ref[b // BY, 0, b % BY]
        own_ref[pl.ds(3 * NB + b, 1), :] = jnp.where(live, strain_ref[b], 0.0)


def strips_kernel(own_ref, other_ref, core_ref, far_ref):
    core = lax.axis_index("core")
    for slot, out in enumerate((core_ref, far_ref)):
        above = (1 - core) if slot == 0 else core
        for layer, ref in enumerate((own_ref, other_ref)):
            for c in range(4):
                out[pl.ds((layer * 4 + c) * BY, BY), :] = ref[pl.ds(c * NB + above * (BX - 1) * BY, BY), :]


def columns_kernel(own_ref, other_ref, core_ref, far_ref, near_out, far_out):
    core, xlo = lax.axis_index("core"), lax.axis_index("xlo")
    for slot, out in enumerate((near_out, far_out)):
        y = ((1 - xlo) if slot == 0 else xlo) * (BY - 1)
        for layer, ref in enumerate((own_ref, other_ref)):
            for c in range(4):
                row, halo = (layer * 4 + c) * WX, (layer * 4 + c) * BY
                out[pl.ds(row + 1, BX), :] = ref[pl.ds(c * NB + y, BX, stride=BY), :]
                out[pl.ds(row + (1 - core) * (WX - 1), 1), :] = core_ref[pl.ds(halo + y, 1), :]
                out[pl.ds(row + core * (WX - 1), 1), :] = far_ref[pl.ds(halo + y, 1), :]


def final_kernel(top_ref, avg_ref, old_ref, own_ref, new_ref, damage_ref):
    highest = jnp.max(top_ref[...], keepdims=True) + 1e-06
    for b in range(0, NB, 12):
        averaged = avg_ref[pl.ds(b, 12), :]
        live = jnp.where(own_ref[pl.ds(3 * NB + b, 12), :] > 0.0, 1.0, 0.0)
        new = jnp.maximum(old_ref[pl.ds(b, 12), 0, :], 4.0 * averaged / highest)
        new_ref[pl.ds(b, 12), 0, :] = new
        damage_ref[pl.ds(b, 12), 0, :] = live * (1.0 - jnp.exp(-(new - 1.0) / 2.5) / new)


def call(kernel, outs, ins, scratch=(), us=1, space=VMEM, extra=()):
    return pl.pallas_call(
        kernel,
        out_shape=tuple(jax.ShapeDtypeStruct(s, d) for s, d in outs),
        in_specs=[space] * ins,
        out_specs=tuple(VMEM for _ in outs),
        scratch_shapes=[pltpu.VMEM(s, d) for s, d in scratch] + list(extra),
        compiler_params=pltpu.CompilerParams(vmem_limit_bytes=16 << 20),
        cost_estimate=pl.CostEstimate(flops=us * 400_000_000, bytes_accessed=1 << 16, transcendentals=0),
        name=kernel.__name__,
    )


def feature_scratch(count):
    return [((count * K, PTS), F32), ((count, PTS), F32), ((count, K, PTS), BF16)]


SUMS = ((2 * NB, PTS), F32)


def on_device(coords, strain, kappa_old, counts, pair_mask):
    raw = (counts.reshape(BX, 1, BY), coords.reshape(3 * NB, 1, PTS), strain.reshape(NB, 1, PTS))
    (own,) = call(
        pack_kernel,
        [((4 * NB, PTS), F32)],
        3,
        space=pl.BlockSpec(memory_space=pltpu.HBM),
        extra=[
            pltpu.SMEM((BX, 1, BY), jnp.int32),
            pltpu.VMEM((3 * NB, 1, PTS), F32),
            pltpu.VMEM((NB, 1, PTS), F32),
            pltpu.SemaphoreType.DMA((3,)),
        ],
    )(*(pltpu.with_memory_space_constraint(v, pltpu.HBM) for v in raw))
    swap = [(0, 1), (1, 0)]
    beside = lambda n: [p for i in range(1, n - 1, 2) for p in ((i, i + 1), (i + 1, i))]
    other = lax.ppermute(own, "ply", swap)
    tile = feature_scratch(NB)
    acc, bcent, flags, own_rows, own_bfeat = call(
        own_kernel,
        [SUMS, ((NB, PTS, K), BF16), ((NB * FLAGS, PTS), F32)] + tile[1:],
        2,
        [((PTS, PTS), F32), ((NB * K, PTS), F32)] + tile[:1],
        6,
    )(pair_mask.reshape(NB, 1, 26), own)

    strip = ((8 * BY, PTS), F32)
    core, far = call(strips_kernel, [strip, strip], 2)(own, other)
    far = lax.ppermute(far, ("y", "core"), beside(8))
    core = lax.ppermute(core, "core", swap)
    acc, rows, bfeat = call(other_kernel, [SUMS] + tile[1:], 4, tile[:1], 3)(other, bcent, flags, acc)

    column = ((8 * WX, PTS), F32)
    ynear, yfar = call(columns_kernel, [column, column], 4)(own, other, core, far)
    yfar = lax.ppermute(yfar, ("z", "xlo"), beside(16))
    ynear = lax.ppermute(ynear, "xlo", swap)
    (acc,) = call(x_kernel, [SUMS], 9, feature_scratch(4 * BY), 4)(
        core, far, bcent, flags, own_rows, own_bfeat, rows, bfeat, acc
    )
    averaged, top = call(y_kernel, [((NB, PTS), F32), ((8, PTS), F32)], 6, feature_scratch(4 * WX) + [SUMS], 2)(
        ynear, yfar, bcent, flags, own, acc
    )

    top = jnp.maximum(top, lax.ppermute(top, "core", swap))
    tops = lax.all_to_all(jnp.broadcast_to(top[:1], (128, PTS)), ("ply", "y", "z", "xlo"), 0, 0, tiled=True)
    new, damage = call(final_kernel, [((NB, 1, PTS), F32)] * 2, 4)(tops, averaged, kappa_old.reshape(NB, 1, PTS), own)
    return (new.reshape(1, BX, BY, PTS), damage.reshape(1, BX, BY, PTS))


def solution(mesh):
    fine = Mesh(mesh.devices.reshape(2, 4, 2, 8, 2), AXES)
    gx, gy = ("y", "core"), ("z", "xlo")
    placed = (
        P(None, "ply", gx, gy, None),
        P("ply", gx, gy, None),
        P("ply", gx, gy, None),
        P("ply", gx, gy),
        P("ply", gx, gy, None),
    )
    return jax.shard_map(
        on_device,
        mesh=fine,
        in_specs=placed,
        out_specs=(P("ply", gx, gy, None), P("ply", gx, gy, None)),
        check_vma=False,
    )
```

```python
import jax
import jax.numpy as jnp
from jax import lax
from jax.experimental import pallas as pl
from jax.experimental.pallas import tpu as pltpu
from jax.sharding import Mesh
from jax.sharding import PartitionSpec as P

BX = 6
BY = 6
NB = BX * BY
WX = BX + 2
PTS = 128
K = 16
FLAGS = 32
AXES = ("ply", "y", "core", "z", "xlo")
F32 = jnp.float32
BF16 = jnp.bfloat16
VMEM = pl.BlockSpec(memory_space=pltpu.VMEM)


def pieces_of(v, count):
    out = []
    for _ in range(count):
        high = v.astype(BF16).astype(F32)
        out.append(high)
        v = v - high
    return out


def positions(ref, row, count, stride, step, x_at, y_at, z_at):
    load = lambda c: ref[pl.ds(row + c * step, count, stride=stride), :]
    shifts = (z_at - 0.5, x_at, y_at)
    pieces = [pieces_of(load(c) + shifts[c], 2) for c in range(3)]
    norm = None
    for high, low in pieces:
        p = high + low
        norm = p * p if norm is None else norm + p * p
    return [p[0] for p in pieces], [p[1] for p in pieces], norm, load(3)


def put_neighbour(feat, rows, base, highs, lows, norm, strain):
    count = strain.shape[0]
    one = jnp.ones_like(strain)
    live = jnp.where(strain > 0.0, 1.0, -256.0)
    listed = highs + lows + highs + pieces_of(live - norm, 3) + [one] * 3 + [jnp.zeros_like(strain)]
    for k, v in enumerate(listed):
        feat[pl.ds(base * K + k, count, stride=K), :] = v
    rows[pl.ds(base, count), :] = strain


def put_center(cent, base, highs, lows, norm):
    count = norm.shape[0]
    one = jnp.ones_like(norm)
    twice = [2.0 * v for v in highs]
    listed = twice + twice + [2.0 * v for v in lows] + [one] * 3 + pieces_of(-norm, 3) + [jnp.zeros_like(norm)]
    for k, v in enumerate(listed):
        cent[pl.ds(base * K + k, count, stride=K), :] = v


def round_tiles(feat, bfeat, count, unroll):
    def one(b, carry):
        bfeat[b] = feat[pl.ds(pl.multiple_of(b * K, K), K), :].astype(BF16)
        return carry

    lax.fori_loop(0, count, one, 0, unroll=unroll)


def pair_sums(center, pairs, bfeat, rows, mask):
    spot = jnp.where(lax.broadcasted_iota(jnp.int32, (K, PTS), 0) == 9, 1.0, 0.0)
    sums = [[None] * 16, [None] * 16]
    for t in range(0, len(pairs), 2):
        some = pairs[t : t + 2]
        tiles = []
        for b, flag in some:
            tile = bfeat[b]
            if flag is not None:
                tile = tile + (spot * jnp.broadcast_to(mask[pl.ds(flag, 1), :], (K, PTS))).astype(BF16)
            tiles.append(tile)
        rhs = jnp.concatenate(tiles, axis=1) if len(tiles) > 1 else tiles[0]
        gap = jnp.dot(center, rhs, preferred_element_type=F32)
        for n, (b, flag) in enumerate(some):
            strain = jnp.broadcast_to(rows[pl.ds(b, 1), :], (8, PTS))
            for r in range(16):
                w = jnp.maximum(gap[r * 8 : r * 8 + 8, n * PTS : (n + 1) * PTS], 0.0)
                w = w * w
                v = w * strain
                sums[0][r] = v if sums[0][r] is None else sums[0][r] + v
                sums[1][r] = w if sums[1][r] is None else sums[1][r] + w
    return [jnp.sum(jnp.concatenate(s, axis=0).T, axis=0, keepdims=True) for s in sums]


def y_in():
    return lax.broadcasted_iota(jnp.int32, (BY, PTS), 0).astype(F32) - (BY // 2)


def flag_row(a, layer, dx, dy):
    t = dx * 3 + dy
    if layer:
        return a * FLAGS + t + jnp.where(lax.axis_index("ply") == 0, 17, 0)
    return a * FLAGS + jnp.where(t == 4, FLAGS - 1, 9 + t - jnp.where(t > 4, 1, 0))


def fill_flags(mask_ref, turned, flags):
    turned[...] = jnp.zeros_like(turned)
    turned[0:NB, 0:26] = (mask_ref[:, 0, :] * 256 - 256).astype(F32)
    across = turned[...].T
    for a in range(NB):
        flags[a * FLAGS : (a + 1) * FLAGS, :] = jnp.broadcast_to(across[0:FLAGS, a : a + 1], (FLAGS, PTS))


def strip_sums(layer, x, first, dxs, bcent, bfeat, rows, flags, acc, add):
    for y in range(BY):
        a = x * BY + y
        pairs = []
        for n in range(dxs):
            for dy in range(3):
                if 0 <= y + dy - 1 < BY:
                    at_self = layer == 0 and dy == 1 and dxs == 3 and n == 1
                    flag = None if at_self else flag_row(a, layer, first + n - x + 1, dy)
                    pairs.append(((first + n) * BY + y + dy - 1, flag))
        for c, s in enumerate(pair_sums(bcent[a], pairs, bfeat, rows, flags)):
            if add:
                s = s + acc[pl.ds(a * 2 + c, 1), :]
            acc[pl.ds(a * 2 + c, 1), :] = s


def edges(layer, add, *refs):
    def edge(e, carry):
        strip_sums(layer, e * (BX - 1), e * (BX - 2), 2, *refs, add)
        return carry

    lax.fori_loop(0, 2, edge, 0, unroll=2)


def middles(layer, low, high, add, unroll, *refs):
    def middle(x, carry):
        strip_sums(layer, x, x - 1, 3, *refs, add)
        return carry

    lax.fori_loop(low, high, middle, 0, unroll=unroll)


def other_shift():
    return (1 - 2 * lax.axis_index("ply")).astype(F32)


def own_kernel(mask_ref, own_ref, acc, bcent, flags, rows, bfeat, turned, cent, feat):
    fill_flags(mask_ref, turned, flags)
    for x in range(BX):
        highs, lows, norm, strain = positions(own_ref, x * BY, BY, 1, NB, float(x - BX // 2), y_in(), 0.0)
        put_neighbour(feat, rows, x * BY, highs, lows, norm, strain)
        put_center(cent, x * BY, highs, lows, norm)
    round_tiles(feat, bfeat, NB, 6)

    def turn(a, carry):
        bcent[a] = cent[pl.ds(pl.multiple_of(a * K, K), K), :].T.astype(BF16)
        return carry

    lax.fori_loop(0, NB, turn, 0, unroll=6)
    refs = (bcent, bfeat, rows, flags, acc)
    edges(0, False, *refs)
    middles(0, 1, BX - 2, False, 3, *refs)
    acc[pl.ds(2 * (BX - 2) * BY, 2 * BY), :] = jnp.zeros((2 * BY, PTS), F32)


def other_kernel(other_ref, bcent, flags, before, acc, rows, bfeat, feat):
    for x in range(BX):
        highs, lows, norm, strain = positions(other_ref, x * BY, BY, 1, NB, float(x - BX // 2), y_in(), other_shift())
        put_neighbour(feat, rows, x * BY, highs, lows, norm, strain)
    round_tiles(feat, bfeat, NB, 6)
    acc[...] = before[...]
    refs = (bcent, bfeat, rows, flags, acc)
    edges(1, True, *refs)
    middles(1, 1, 2, True, 1, *refs)


def x_kernel(
    core_ref, far_ref, bcent, flags, own_rows, own_bfeat, other_rows, other_bfeat, before, acc, feat, rows, bfeat
):
    core = lax.axis_index("core")
    for slot, ref in enumerate((core_ref, far_ref)):
        above = (1 - core) if slot == 0 else core
        x_at = (above * (BX + 1) - 1 - BX // 2).astype(F32)
        for layer in range(2):
            highs, lows, norm, strain = positions(
                ref, layer * 4 * BY, BY, 1, BY, x_at, y_in(), other_shift() if layer else 0.0
            )
            put_neighbour(feat, rows, (slot * 2 + layer) * BY, highs, lows, norm, strain)
    round_tiles(feat, bfeat, 4 * BY, 6)
    acc[...] = before[...]

    def side(slot, carry):
        above = jnp.where(slot == 0, 1 - core, core)
        for y in range(BY):
            a = above * (BX - 1) * BY + y
            pairs = [
                ((slot * 2 + layer) * BY + y + dy - 1, flag_row(a, layer, above * 2, dy))
                for layer in range(2)
                for dy in range(3)
                if 0 <= y + dy - 1 < BY
            ]
            for c, s in enumerate(pair_sums(bcent[a], pairs, bfeat, rows, flags)):
                acc[pl.ds(a * 2 + c, 1), :] += s
        return carry

    lax.fori_loop(0, 2, side, 0, unroll=2)
    middles(0, BX - 2, BX - 1, True, 1, bcent, own_bfeat, own_rows, flags, acc)
    middles(1, 2, BX - 1, True, 3, bcent, other_bfeat, other_rows, flags, acc)


def y_kernel(near_ref, far_ref, bcent, flags, own_ref, before, avg_ref, top_ref, feat, rows, bfeat, acc):
    xlo = lax.axis_index("xlo")
    acc[...] = before[...]
    x_in = lax.broadcasted_iota(jnp.int32, (WX, PTS), 0).astype(F32) - (WX // 2)
    for slot, ref in enumerate((near_ref, far_ref)):
        above = (1 - xlo) if slot == 0 else xlo
        y_at = (above * (BY + 1) - 1 - BY // 2).astype(F32)
        for layer in range(2):
            highs, lows, norm, strain = positions(
                ref, layer * 4 * WX, WX, 1, WX, x_in, y_at, other_shift() if layer else 0.0
            )
            put_neighbour(feat, rows, (slot * 2 + layer) * WX, highs, lows, norm, strain)
    round_tiles(feat, bfeat, 4 * WX, 8)

    def side(slot, carry):
        above = jnp.where(slot == 0, 1 - xlo, xlo)
        for x in range(BX):
            a = above * (BY - 1) + x * BY
            pairs = [
                ((slot * 2 + layer) * WX + x + dx, flag_row(a, layer, dx, above * 2))
                for layer in range(2)
                for dx in range(3)
            ]
            for c, s in enumerate(pair_sums(bcent[a], pairs, bfeat, rows, flags)):
                acc[pl.ds(a * 2 + c, 1), :] += s
        return carry

    lax.fori_loop(0, 2, side, 0, unroll=2)
    top = None
    for r in range(0, NB, 12):
        s = [acc[pl.ds(r * 2 + k, 12, stride=2), :] for k in range(2)]
        live = jnp.where(own_ref[pl.ds(3 * NB + r, 12), :] > 0.0, 1.0, 0.0)
        averaged = live * s[0] / (s[1] + 1.0 - live)
        avg_ref[pl.ds(r, 12), :] = averaged
        top = averaged if top is None else jnp.maximum(top, averaged)
    top_ref[...] = jnp.broadcast_to(jnp.max(top, axis=0, keepdims=True), (8, PTS))


def pack_kernel(counts_hbm, coords_hbm, strain_hbm, own_ref, counts_ref, coords_ref, strain_ref, sems):
    copies = [
        pltpu.make_async_copy(source, target, sems.at[n])
        for n, (source, target) in enumerate(
            ((counts_hbm, counts_ref), (strain_hbm, strain_ref), (coords_hbm, coords_ref))
        )
    ]
    for copy in copies:
        copy.start()
    for copy in copies:
        copy.wait()
    slots = lax.broadcasted_iota(jnp.int32, (1, PTS), 1)
    for c in range(3):
        own_ref[pl.ds(c * NB, NB), :] = coords_ref[pl.ds(c * NB, NB), 0, :]
    for b in range(NB):
        live = slots < counts_ref[b // BY, 0, b % BY]
        own_ref[pl.ds(3 * NB + b, 1), :] = jnp.where(live, strain_ref[b], 0.0)


def strips_kernel(own_ref, other_ref, core_ref, far_ref):
    core = lax.axis_index("core")
    for slot, out in enumerate((core_ref, far_ref)):
        above = (1 - core) if slot == 0 else core
        for layer, ref in enumerate((own_ref, other_ref)):
            for c in range(4):
                out[pl.ds((layer * 4 + c) * BY, BY), :] = ref[pl.ds(c * NB + above * (BX - 1) * BY, BY), :]


def columns_kernel(own_ref, other_ref, core_ref, far_ref, near_out, far_out):
    core, xlo = lax.axis_index("core"), lax.axis_index("xlo")
    for slot, out in enumerate((near_out, far_out)):
        y = ((1 - xlo) if slot == 0 else xlo) * (BY - 1)
        for layer, ref in enumerate((own_ref, other_ref)):
            for c in range(4):
                row, halo = (layer * 4 + c) * WX, (layer * 4 + c) * BY
                out[pl.ds(row + 1, BX), :] = ref[pl.ds(c * NB + y, BX, stride=BY), :]
                out[pl.ds(row + (1 - core) * (WX - 1), 1), :] = core_ref[pl.ds(halo + y, 1), :]
                out[pl.ds(row + core * (WX - 1), 1), :] = far_ref[pl.ds(halo + y, 1), :]


def final_kernel(top_ref, avg_ref, old_ref, own_ref, new_ref, damage_ref):
    highest = jnp.max(top_ref[...], keepdims=True) + 1e-06
    for b in range(0, NB, 12):
        averaged = avg_ref[pl.ds(b, 12), :]
        live = jnp.where(own_ref[pl.ds(3 * NB + b, 12), :] > 0.0, 1.0, 0.0)
        new = jnp.maximum(old_ref[pl.ds(b, 12), 0, :], 4.0 * averaged / highest)
        new_ref[pl.ds(b, 12), 0, :] = new
        damage_ref[pl.ds(b, 12), 0, :] = live * (1.0 - jnp.exp(-(new - 1.0) / 2.5) / new)


def call(kernel, outs, ins, scratch=(), us=1, space=VMEM, extra=()):
    return pl.pallas_call(
        kernel,
        out_shape=tuple(jax.ShapeDtypeStruct(s, d) for s, d in outs),
        in_specs=[space] * ins,
        out_specs=tuple(VMEM for _ in outs),
        scratch_shapes=[pltpu.VMEM(s, d) for s, d in scratch] + list(extra),
        compiler_params=pltpu.CompilerParams(vmem_limit_bytes=16 << 20),
        cost_estimate=pl.CostEstimate(flops=us * 400_000_000, bytes_accessed=1 << 16, transcendentals=0),
    )


def feature_scratch(count):
    return [((count * K, PTS), F32), ((count, PTS), F32), ((count, K, PTS), BF16)]


SUMS = ((2 * NB, PTS), F32)


def on_device(coords, strain, kappa_old, counts, pair_mask):
    raw = (counts.reshape(BX, 1, BY), coords.reshape(3 * NB, 1, PTS), strain.reshape(NB, 1, PTS))
    (own,) = call(
        pack_kernel,
        [((4 * NB, PTS), F32)],
        3,
        space=pl.BlockSpec(memory_space=pltpu.HBM),
        extra=[
            pltpu.SMEM((BX, 1, BY), jnp.int32),
            pltpu.VMEM((3 * NB, 1, PTS), F32),
            pltpu.VMEM((NB, 1, PTS), F32),
            pltpu.SemaphoreType.DMA((3,)),
        ],
    )(*(pltpu.with_memory_space_constraint(v, pltpu.HBM) for v in raw))
    swap = [(0, 1), (1, 0)]
    beside = lambda n: [p for i in range(1, n - 1, 2) for p in ((i, i + 1), (i + 1, i))]
    other = lax.ppermute(own, "ply", swap)
    tile = feature_scratch(NB)
    acc, bcent, flags, own_rows, own_bfeat = call(
        own_kernel,
        [SUMS, ((NB, PTS, K), BF16), ((NB * FLAGS, PTS), F32)] + tile[1:],
        2,
        [((PTS, PTS), F32), ((NB * K, PTS), F32)] + tile[:1],
        6,
    )(pair_mask.reshape(NB, 1, 26), own)

    strip = ((8 * BY, PTS), F32)
    core, far = call(strips_kernel, [strip, strip], 2)(own, other)
    far = lax.ppermute(far, ("y", "core"), beside(8))
    core = lax.ppermute(core, "core", swap)
    acc, rows, bfeat = call(other_kernel, [SUMS] + tile[1:], 4, tile[:1], 3)(other, bcent, flags, acc)

    column = ((8 * WX, PTS), F32)
    ynear, yfar = call(columns_kernel, [column, column], 4)(own, other, core, far)
    yfar = lax.ppermute(yfar, ("z", "xlo"), beside(16))
    ynear = lax.ppermute(ynear, "xlo", swap)
    (acc,) = call(x_kernel, [SUMS], 9, feature_scratch(4 * BY), 4)(
        core, far, bcent, flags, own_rows, own_bfeat, rows, bfeat, acc
    )
    averaged, top = call(y_kernel, [((NB, PTS), F32), ((8, PTS), F32)], 6, feature_scratch(4 * WX) + [SUMS], 2)(
        ynear, yfar, bcent, flags, own, acc
    )

    tops = lax.all_to_all(jnp.broadcast_to(top[:1], (256, PTS)), AXES, 0, 0, tiled=True)
    new, damage = call(final_kernel, [((NB, 1, PTS), F32)] * 2, 4)(tops, averaged, kappa_old.reshape(NB, 1, PTS), own)
    return (new.reshape(1, BX, BY, PTS), damage.reshape(1, BX, BY, PTS))


def solution(mesh):
    fine = Mesh(mesh.devices.reshape(2, 4, 2, 8, 2), AXES)
    gx, gy = ("y", "core"), ("z", "xlo")
    placed = (
        P(None, "ply", gx, gy, None),
        P("ply", gx, gy, None),
        P("ply", gx, gy, None),
        P("ply", gx, gy),
        P("ply", gx, gy, None),
    )

    return jax.shard_map(
        on_device,
        mesh=fine,
        in_specs=placed,
        out_specs=(P("ply", gx, gy, None), P("ply", gx, gy, None)),
        check_vma=False,
    )
```

```python
import jax
import jax.numpy as jnp
from jax import lax
from jax.experimental import pallas as pl
from jax.experimental.pallas import tpu as pltpu
from jax.sharding import Mesh
from jax.sharding import PartitionSpec as P

BX = 6
BY = 6
NB = BX * BY
WX = BX + 2
PTS = 128
K = 16
MID = NB - 2 * BY
FLAGS = 32
AXES = ("ply", "y", "core", "z", "xlo")
F32 = jnp.float32
BF16 = jnp.bfloat16
VMEM = pl.BlockSpec(memory_space=pltpu.VMEM)


def pieces_of(v, count):
    out = []
    for _ in range(count):
        high = v.astype(BF16).astype(F32)
        out.append(high)
        v = v - high
    return out


def positions(ref, row, count, stride, step, x_at, y_at, z_at):
    load = lambda c: ref[pl.ds(row + c * step, count, stride=stride), :]
    shifts = (z_at - 0.5, x_at, y_at)
    pieces = [pieces_of(load(c) + shifts[c], 2) for c in range(3)]
    norm = None
    for high, low in pieces:
        p = high + low
        norm = p * p if norm is None else norm + p * p
    return [p[0] for p in pieces], [p[1] for p in pieces], norm, load(3)


def put_neighbour(feat, rows, base, highs, lows, norm, strain):
    count = strain.shape[0]
    one = jnp.ones_like(strain)
    live = jnp.where(strain > 0.0, 1.0, -256.0)
    listed = highs + lows + highs + pieces_of(live - norm, 3) + [one] * 3 + [jnp.zeros_like(strain)]
    for k, v in enumerate(listed):
        feat[pl.ds(base * K + k, count, stride=K), :] = v
    rows[pl.ds(base, count), :] = strain


def put_center(cent, base, highs, lows, norm):
    count = norm.shape[0]
    one = jnp.ones_like(norm)
    twice = [2.0 * v for v in highs]
    listed = twice + twice + [2.0 * v for v in lows] + [one] * 3 + pieces_of(-norm, 3) + [jnp.zeros_like(norm)]
    for k, v in enumerate(listed):
        cent[pl.ds(base * K + k, count, stride=K), :] = v


def round_tiles(feat, bfeat, count, unroll):
    def one(b, carry):
        bfeat[b] = feat[pl.ds(pl.multiple_of(b * K, K), K), :].astype(BF16)
        return carry

    lax.fori_loop(0, count, one, 0, unroll=unroll)


def pair_sums(center, pairs, bfeat, rows, mask):
    spot = jnp.where(lax.broadcasted_iota(jnp.int32, (K, PTS), 0) == 9, 1.0, 0.0)
    sums = [[None] * 16, [None] * 16]
    for t in range(0, len(pairs), 2):
        some = pairs[t : t + 2]
        tiles = []
        for b, flag in some:
            tile = bfeat[b]
            if flag is not None:
                tile = tile + (spot * jnp.broadcast_to(mask[pl.ds(flag, 1), :], (K, PTS))).astype(BF16)
            tiles.append(tile)
        rhs = jnp.concatenate(tiles, axis=1) if len(tiles) > 1 else tiles[0]
        gap = jnp.dot(center, rhs, preferred_element_type=F32)
        for n, (b, flag) in enumerate(some):
            strain = jnp.broadcast_to(rows[pl.ds(b, 1), :], (8, PTS))
            for r in range(16):
                w = jnp.maximum(gap[r * 8 : r * 8 + 8, n * PTS : (n + 1) * PTS], 0.0)
                w = w * w
                v = w * strain
                sums[0][r] = v if sums[0][r] is None else sums[0][r] + v
                sums[1][r] = w if sums[1][r] is None else sums[1][r] + w
    return [jnp.sum(jnp.concatenate(s, axis=0).T, axis=0, keepdims=True) for s in sums]


def y_in():
    return lax.broadcasted_iota(jnp.int32, (BY, PTS), 0).astype(F32) - (BY // 2)


def flag_row(a, layer, dx, dy):
    t = dx * 3 + dy
    if layer:
        return a * FLAGS + t + jnp.where(lax.axis_index("ply") == 0, 17, 0)
    return a * FLAGS + jnp.where(t == 4, FLAGS - 1, 9 + t - jnp.where(t > 4, 1, 0))


def fill_flags(mask_ref, turned, flags):
    turned[...] = jnp.zeros_like(turned)
    turned[0:NB, 0:26] = (mask_ref[:, 0, :] * 256 - 256).astype(F32)
    across = turned[...].T
    for a in range(NB):
        flags[a * FLAGS : (a + 1) * FLAGS, :] = jnp.broadcast_to(across[0:FLAGS, a : a + 1], (FLAGS, PTS))


def strip_sums(layer, x, first, dxs, bcent, bfeat, rows, flags, acc, add):
    for y in range(BY):
        a = x * BY + y
        pairs = []
        for n in range(dxs):
            for dy in range(3):
                if 0 <= y + dy - 1 < BY:
                    at_self = layer == 0 and dy == 1 and dxs == 3 and n == 1
                    flag = None if at_self else flag_row(a, layer, first + n - x + 1, dy)
                    pairs.append(((first + n) * BY + y + dy - 1, flag))
        for c, s in enumerate(pair_sums(bcent[a], pairs, bfeat, rows, flags)):
            if add:
                s = s + acc[pl.ds(a * 2 + c, 1), :]
            acc[pl.ds(a * 2 + c, 1), :] = s


def edges(layer, add, *refs):
    def edge(e, carry):
        strip_sums(layer, e * (BX - 1), e * (BX - 2), 2, *refs, add)
        return carry

    lax.fori_loop(0, 2, edge, 0, unroll=2)


def middles(layer, low, high, add, unroll, *refs):
    def middle(x, carry):
        strip_sums(layer, x, x - 1, 3, *refs, add)
        return carry

    lax.fori_loop(low, high, middle, 0, unroll=unroll)


def other_shift():
    return (1 - 2 * lax.axis_index("ply")).astype(F32)


def own_kernel(mask_ref, own_ref, acc, bcent, flags, rows, bfeat, turned, cent, feat):
    fill_flags(mask_ref, turned, flags)
    for x in range(BX):
        highs, lows, norm, strain = positions(own_ref, x * BY, BY, 1, NB, float(x - BX // 2), y_in(), 0.0)
        put_neighbour(feat, rows, x * BY, highs, lows, norm, strain)
        put_center(cent, x * BY, highs, lows, norm)
    round_tiles(feat, bfeat, NB, 6)

    def turn(a, carry):
        bcent[a] = cent[pl.ds(pl.multiple_of(a * K, K), K), :].T.astype(BF16)
        return carry

    lax.fori_loop(0, NB, turn, 0, unroll=6)
    refs = (bcent, bfeat, rows, flags, acc)
    edges(0, False, *refs)
    middles(0, 1, BX - 2, False, 3, *refs)
    acc[pl.ds(2 * (BX - 2) * BY, 2 * BY), :] = jnp.zeros((2 * BY, PTS), F32)


def other_kernel(edge_ref, mid_ref, bcent, flags, before, acc, rows, bfeat, feat):
    for x in range(BX):
        if x in (0, BX - 1):
            place = (edge_ref, min(x, 1) * BY, BY, 1, 2 * BY)
        else:
            place = (mid_ref, (x - 1) * BY, BY, 1, MID)
        highs, lows, norm, strain = positions(*place, float(x - BX // 2), y_in(), other_shift())
        put_neighbour(feat, rows, x * BY, highs, lows, norm, strain)
    round_tiles(feat, bfeat, NB, 6)
    acc[...] = before[...]
    refs = (bcent, bfeat, rows, flags, acc)
    edges(1, True, *refs)
    middles(1, 1, 2, True, 1, *refs)


def x_kernel(
    core_ref, far_ref, bcent, flags, own_rows, own_bfeat, other_rows, other_bfeat, before, acc, feat, rows, bfeat
):
    core = lax.axis_index("core")
    for slot, ref in enumerate((core_ref, far_ref)):
        above = (1 - core) if slot == 0 else core
        x_at = (above * (BX + 1) - 1 - BX // 2).astype(F32)
        for layer in range(2):
            highs, lows, norm, strain = positions(
                ref, layer * 4 * BY, BY, 1, BY, x_at, y_in(), other_shift() if layer else 0.0
            )
            put_neighbour(feat, rows, (slot * 2 + layer) * BY, highs, lows, norm, strain)
    round_tiles(feat, bfeat, 4 * BY, 6)
    acc[...] = before[...]

    def side(slot, carry):
        above = jnp.where(slot == 0, 1 - core, core)
        for y in range(BY):
            a = above * (BX - 1) * BY + y
            pairs = [
                ((slot * 2 + layer) * BY + y + dy - 1, flag_row(a, layer, above * 2, dy))
                for layer in range(2)
                for dy in range(3)
                if 0 <= y + dy - 1 < BY
            ]
            for c, s in enumerate(pair_sums(bcent[a], pairs, bfeat, rows, flags)):
                acc[pl.ds(a * 2 + c, 1), :] += s
        return carry

    lax.fori_loop(0, 2, side, 0, unroll=2)
    middles(0, BX - 2, BX - 1, True, 1, bcent, own_bfeat, own_rows, flags, acc)
    middles(1, 2, BX - 1, True, 3, bcent, other_bfeat, other_rows, flags, acc)


def y_kernel(near_ref, far_ref, bcent, flags, own_ref, before, avg_ref, top_ref, feat, rows, bfeat, acc):
    xlo = lax.axis_index("xlo")
    acc[...] = before[...]
    x_in = lax.broadcasted_iota(jnp.int32, (WX, PTS), 0).astype(F32) - (WX // 2)
    for slot, ref in enumerate((near_ref, far_ref)):
        above = (1 - xlo) if slot == 0 else xlo
        y_at = (above * (BY + 1) - 1 - BY // 2).astype(F32)
        for layer in range(2):
            highs, lows, norm, strain = positions(
                ref, layer * 4 * WX, WX, 1, WX, x_in, y_at, other_shift() if layer else 0.0
            )
            put_neighbour(feat, rows, (slot * 2 + layer) * WX, highs, lows, norm, strain)
    round_tiles(feat, bfeat, 4 * WX, 8)

    def side(slot, carry):
        above = jnp.where(slot == 0, 1 - xlo, xlo)
        for x in range(BX):
            a = above * (BY - 1) + x * BY
            pairs = [
                ((slot * 2 + layer) * WX + x + dx, flag_row(a, layer, dx, above * 2))
                for layer in range(2)
                for dx in range(3)
            ]
            for c, s in enumerate(pair_sums(bcent[a], pairs, bfeat, rows, flags)):
                acc[pl.ds(a * 2 + c, 1), :] += s
        return carry

    lax.fori_loop(0, 2, side, 0, unroll=2)
    top = None
    for r in range(0, NB, 12):
        s = [acc[pl.ds(r * 2 + k, 12, stride=2), :] for k in range(2)]
        live = jnp.where(own_ref[pl.ds(3 * NB + r, 12), :] > 0.0, 1.0, 0.0)
        averaged = live * s[0] / (s[1] + 1.0 - live)
        avg_ref[pl.ds(r, 12), :] = averaged
        top = averaged if top is None else jnp.maximum(top, averaged)
    top_ref[...] = jnp.broadcast_to(jnp.max(top, axis=0, keepdims=True), (8, PTS))


def pack_kernel(counts_hbm, coords_hbm, strain_hbm, own_ref, edge_ref, mid_ref, counts_ref, coords_ref, strain_ref, sems):
    copies = [
        pltpu.make_async_copy(source, target, sems.at[n])
        for n, (source, target) in enumerate(
            ((counts_hbm, counts_ref), (strain_hbm, strain_ref), (coords_hbm, coords_ref))
        )
    ]
    for copy in copies:
        copy.start()
    for copy in copies:
        copy.wait()
    slots = lax.broadcasted_iota(jnp.int32, (1, PTS), 1)
    for c in range(3):
        own_ref[pl.ds(c * NB, NB), :] = coords_ref[pl.ds(c * NB, NB), 0, :]
    for b in range(NB):
        live = slots < counts_ref[b // BY, 0, b % BY]
        own_ref[pl.ds(3 * NB + b, 1), :] = jnp.where(live, strain_ref[b], 0.0)
    for c in range(4):
        edge_ref[pl.ds(c * 2 * BY, BY), :] = own_ref[pl.ds(c * NB, BY), :]
        edge_ref[pl.ds(c * 2 * BY + BY, BY), :] = own_ref[pl.ds(c * NB + NB - BY, BY), :]
        mid_ref[pl.ds(c * MID, MID), :] = own_ref[pl.ds(c * NB + BY, MID), :]


def strips_kernel(own_edge_ref, other_edge_ref, core_ref, far_ref):
    core = lax.axis_index("core")
    for slot, out in enumerate((core_ref, far_ref)):
        above = (1 - core) if slot == 0 else core
        for layer, ref in enumerate((own_edge_ref, other_edge_ref)):
            for c in range(4):
                out[pl.ds((layer * 4 + c) * BY, BY), :] = ref[pl.ds((c * 2 + above) * BY, BY), :]


def columns_kernel(own_edge_ref, own_mid_ref, other_edge_ref, other_mid_ref, core_ref, far_ref, near_out, far_out):
    core, xlo = lax.axis_index("core"), lax.axis_index("xlo")
    for slot, out in enumerate((near_out, far_out)):
        y = ((1 - xlo) if slot == 0 else xlo) * (BY - 1)
        for layer, (edge, mid) in enumerate(((own_edge_ref, own_mid_ref), (other_edge_ref, other_mid_ref))):
            for c in range(4):
                row, halo = (layer * 4 + c) * WX, (layer * 4 + c) * BY
                out[pl.ds(row + 1, 1), :] = edge[pl.ds(c * 2 * BY + y, 1), :]
                out[pl.ds(row + 2, BX - 2), :] = mid[pl.ds(c * MID + y, BX - 2, stride=BY), :]
                out[pl.ds(row + BX, 1), :] = edge[pl.ds(c * 2 * BY + BY + y, 1), :]
                out[pl.ds(row + (1 - core) * (WX - 1), 1), :] = core_ref[pl.ds(halo + y, 1), :]
                out[pl.ds(row + core * (WX - 1), 1), :] = far_ref[pl.ds(halo + y, 1), :]


def final_kernel(top_ref, avg_ref, old_ref, own_ref, new_ref, damage_ref):
    highest = jnp.max(top_ref[...], keepdims=True) + 1e-06
    for b in range(0, NB, 12):
        averaged = avg_ref[pl.ds(b, 12), :]
        live = jnp.where(own_ref[pl.ds(3 * NB + b, 12), :] > 0.0, 1.0, 0.0)
        new = jnp.maximum(old_ref[pl.ds(b, 12), 0, :], 4.0 * averaged / highest)
        new_ref[pl.ds(b, 12), 0, :] = new
        damage_ref[pl.ds(b, 12), 0, :] = live * (1.0 - jnp.exp(-(new - 1.0) / 2.5) / new)


def call(kernel, outs, ins, scratch=(), us=1, space=VMEM, extra=()):
    return pl.pallas_call(
        kernel,
        out_shape=tuple(jax.ShapeDtypeStruct(s, d) for s, d in outs),
        in_specs=[space] * ins,
        out_specs=tuple(VMEM for _ in outs),
        scratch_shapes=[pltpu.VMEM(s, d) for s, d in scratch] + list(extra),
        compiler_params=pltpu.CompilerParams(vmem_limit_bytes=16 << 20),
        cost_estimate=pl.CostEstimate(flops=us * 400_000_000, bytes_accessed=1 << 16, transcendentals=0),
    )


def feature_scratch(count):
    return [((count * K, PTS), F32), ((count, PTS), F32), ((count, K, PTS), BF16)]


SUMS = ((2 * NB, PTS), F32)


def on_device(coords, strain, kappa_old, counts, pair_mask):
    raw = (counts.reshape(BX, 1, BY), coords.reshape(3 * NB, 1, PTS), strain.reshape(NB, 1, PTS))
    own, own_edge, own_mid = call(
        pack_kernel,
        [((4 * NB, PTS), F32), ((8 * BY, PTS), F32), ((4 * MID, PTS), F32)],
        3,
        space=pl.BlockSpec(memory_space=pltpu.HBM),
        extra=[
            pltpu.SMEM((BX, 1, BY), jnp.int32),
            pltpu.VMEM((3 * NB, 1, PTS), F32),
            pltpu.VMEM((NB, 1, PTS), F32),
            pltpu.SemaphoreType.DMA((3,)),
        ],
    )(*(pltpu.with_memory_space_constraint(v, pltpu.HBM) for v in raw))
    swap = [(0, 1), (1, 0)]
    beside = lambda n: [p for i in range(1, n - 1, 2) for p in ((i, i + 1), (i + 1, i))]
    other_edge = lax.ppermute(own_edge, "ply", swap)
    other_mid = lax.ppermute(own_mid, "ply", swap)
    tile = feature_scratch(NB)
    acc, bcent, flags, own_rows, own_bfeat = call(
        own_kernel,
        [SUMS, ((NB, PTS, K), BF16), ((NB * FLAGS, PTS), F32)] + tile[1:],
        2,
        [((PTS, PTS), F32), ((NB * K, PTS), F32)] + tile[:1],
        6,
    )(pair_mask.reshape(NB, 1, 26), own)

    strip = ((8 * BY, PTS), F32)
    core, far = call(strips_kernel, [strip, strip], 2)(own_edge, other_edge)
    far = lax.ppermute(far, ("y", "core"), beside(8))
    core = lax.ppermute(core, "core", swap)
    acc, rows, bfeat = call(other_kernel, [SUMS] + tile[1:], 5, tile[:1], 3)(other_edge, other_mid, bcent, flags, acc)

    column = ((8 * WX, PTS), F32)
    ynear, yfar = call(columns_kernel, [column, column], 6)(own_edge, own_mid, other_edge, other_mid, core, far)
    yfar = lax.ppermute(yfar, ("z", "xlo"), beside(16))
    ynear = lax.ppermute(ynear, "xlo", swap)
    (acc,) = call(x_kernel, [SUMS], 9, feature_scratch(4 * BY), 4)(
        core, far, bcent, flags, own_rows, own_bfeat, rows, bfeat, acc
    )
    averaged, top = call(y_kernel, [((NB, PTS), F32), ((8, PTS), F32)], 6, feature_scratch(4 * WX) + [SUMS], 2)(
        ynear, yfar, bcent, flags, own, acc
    )

    tops = lax.all_to_all(jnp.broadcast_to(top[:1], (256, PTS)), AXES, 0, 0, tiled=True)
    new, damage = call(final_kernel, [((NB, 1, PTS), F32)] * 2, 4)(tops, averaged, kappa_old.reshape(NB, 1, PTS), own)
    return (new.reshape(1, BX, BY, PTS), damage.reshape(1, BX, BY, PTS))


def solution(mesh):
    fine = Mesh(mesh.devices.reshape(2, 4, 2, 8, 2), AXES)
    gx, gy = ("y", "core"), ("z", "xlo")
    placed = (
        P(None, "ply", gx, gy, None),
        P("ply", gx, gy, None),
        P("ply", gx, gy, None),
        P("ply", gx, gy),
        P("ply", gx, gy, None),
    )

    return jax.shard_map(
        on_device,
        mesh=fine,
        in_specs=placed,
        out_specs=(P("ply", gx, gy, None), P("ply", gx, gy, None)),
        check_vma=False,
    )
```

```python
import jax
import jax.numpy as jnp
from jax import lax
from jax.experimental import pallas as pl
from jax.experimental.pallas import tpu as pltpu
from jax.sharding import Mesh
from jax.sharding import PartitionSpec as P

BX = 6
BY = 6
NB = BX * BY
WX = BX + 2
PTS = 128
K = 16
FLAGS = 32
AXES = ("ply", "y", "core", "z", "xlo")
F32 = jnp.float32
BF16 = jnp.bfloat16
VMEM = pl.BlockSpec(memory_space=pltpu.VMEM)


def pieces_of(v, count):
    out = []
    for _ in range(count):
        high = v.astype(BF16).astype(F32)
        out.append(high)
        v = v - high
    return out


def positions(ref, row, count, stride, step, x_at, y_at, z_at):
    load = lambda c: ref[pl.ds(row + c * step, count, stride=stride), :]
    shifts = (z_at - 0.5, x_at, y_at)
    pieces = [pieces_of(load(c) + shifts[c], 2) for c in range(3)]
    norm = None
    for high, low in pieces:
        p = high + low
        norm = p * p if norm is None else norm + p * p
    return [p[0] for p in pieces], [p[1] for p in pieces], norm, load(3)


def put_neighbour(feat, rows, base, highs, lows, norm, strain):
    count = strain.shape[0]
    one = jnp.ones_like(strain)
    live = jnp.where(strain > 0.0, 1.0, -256.0)
    listed = highs + lows + highs + pieces_of(live - norm, 3) + [one] * 3 + [jnp.zeros_like(strain)]
    for k, v in enumerate(listed):
        feat[pl.ds(base * K + k, count, stride=K), :] = v
    rows[pl.ds(base, count), :] = strain


def put_center(cent, base, highs, lows, norm):
    count = norm.shape[0]
    one = jnp.ones_like(norm)
    twice = [2.0 * v for v in highs]
    listed = twice + twice + [2.0 * v for v in lows] + [one] * 3 + pieces_of(-norm, 3) + [jnp.zeros_like(norm)]
    for k, v in enumerate(listed):
        cent[pl.ds(base * K + k, count, stride=K), :] = v


def round_tiles(feat, bfeat, count, unroll):
    def one(b, carry):
        bfeat[b] = feat[pl.ds(pl.multiple_of(b * K, K), K), :].astype(BF16)
        return carry

    lax.fori_loop(0, count, one, 0, unroll=unroll)


def pair_sums(center, pairs, bfeat, rows, mask):
    spot = jnp.where(lax.broadcasted_iota(jnp.int32, (K, PTS), 0) == 9, 1.0, 0.0)
    sums = [[None] * 16, [None] * 16]
    for t in range(0, len(pairs), 2):
        some = pairs[t : t + 2]
        tiles = []
        for b, flag in some:
            tile = bfeat[b]
            if flag is not None:
                tile = tile + (spot * jnp.broadcast_to(mask[pl.ds(flag, 1), :], (K, PTS))).astype(BF16)
            tiles.append(tile)
        rhs = jnp.concatenate(tiles, axis=1) if len(tiles) > 1 else tiles[0]
        gap = jnp.dot(center, rhs, preferred_element_type=F32)
        for n, (b, flag) in enumerate(some):
            strain = jnp.broadcast_to(rows[pl.ds(b, 1), :], (8, PTS))
            for r in range(16):
                w = jnp.maximum(gap[r * 8 : r * 8 + 8, n * PTS : (n + 1) * PTS], 0.0)
                w = w * w
                v = w * strain
                sums[0][r] = v if sums[0][r] is None else sums[0][r] + v
                sums[1][r] = w if sums[1][r] is None else sums[1][r] + w
    return [jnp.sum(jnp.concatenate(s, axis=0).T, axis=0, keepdims=True) for s in sums]


def y_in():
    return lax.broadcasted_iota(jnp.int32, (BY, PTS), 0).astype(F32) - (BY // 2)


def flag_row(a, layer, dx, dy):
    t = dx * 3 + dy
    if layer:
        return a * FLAGS + t + jnp.where(lax.axis_index("ply") == 0, 17, 0)
    return a * FLAGS + jnp.where(t == 4, FLAGS - 1, 9 + t - jnp.where(t > 4, 1, 0))


def fill_flags(mask_ref, turned, flags):
    turned[...] = jnp.zeros_like(turned)
    turned[0:NB, 0:26] = (mask_ref[:, 0, :] * 256 - 256).astype(F32)
    across = turned[...].T
    for a in range(NB):
        flags[a * FLAGS : (a + 1) * FLAGS, :] = jnp.broadcast_to(across[0:FLAGS, a : a + 1], (FLAGS, PTS))


def strip_sums(layer, x, first, dxs, bcent, bfeat, rows, flags, acc, add):
    for y in range(BY):
        a = x * BY + y
        pairs = []
        for n in range(dxs):
            for dy in range(3):
                if 0 <= y + dy - 1 < BY:
                    at_self = layer == 0 and dy == 1 and dxs == 3 and n == 1
                    flag = None if at_self else flag_row(a, layer, first + n - x + 1, dy)
                    pairs.append(((first + n) * BY + y + dy - 1, flag))
        for c, s in enumerate(pair_sums(bcent[a], pairs, bfeat, rows, flags)):
            if add:
                s = s + acc[pl.ds(a * 2 + c, 1), :]
            acc[pl.ds(a * 2 + c, 1), :] = s


def edges(layer, add, *refs):
    def edge(e, carry):
        strip_sums(layer, e * (BX - 1), e * (BX - 2), 2, *refs, add)
        return carry

    lax.fori_loop(0, 2, edge, 0, unroll=2)


def middles(layer, low, high, add, unroll, *refs):
    def middle(x, carry):
        strip_sums(layer, x, x - 1, 3, *refs, add)
        return carry

    lax.fori_loop(low, high, middle, 0, unroll=unroll)


def other_shift():
    return (1 - 2 * lax.axis_index("ply")).astype(F32)


def own_kernel(mask_ref, own_ref, acc, bcent, flags, turned, cent, feat, rows, bfeat):
    fill_flags(mask_ref, turned, flags)
    for x in range(BX):
        highs, lows, norm, strain = positions(own_ref, x * BY, BY, 1, NB, float(x - BX // 2), y_in(), 0.0)
        put_neighbour(feat, rows, x * BY, highs, lows, norm, strain)
        put_center(cent, x * BY, highs, lows, norm)
    round_tiles(feat, bfeat, NB, 6)

    def turn(a, carry):
        bcent[a] = cent[pl.ds(pl.multiple_of(a * K, K), K), :].T.astype(BF16)
        return carry

    lax.fori_loop(0, NB, turn, 0, unroll=6)
    refs = (bcent, bfeat, rows, flags, acc)
    edges(0, False, *refs)
    middles(0, 1, BX - 1, False, 2, *refs)


def other_kernel(other_ref, bcent, flags, before, acc, rows, bfeat, feat):
    for x in range(BX):
        highs, lows, norm, strain = positions(other_ref, x * BY, BY, 1, NB, float(x - BX // 2), y_in(), other_shift())
        put_neighbour(feat, rows, x * BY, highs, lows, norm, strain)
    round_tiles(feat, bfeat, NB, 6)
    acc[...] = before[...]
    refs = (bcent, bfeat, rows, flags, acc)
    edges(1, True, *refs)
    middles(1, 1, 2, True, 1, *refs)


def x_kernel(
    core_ref, far_ref, bcent, flags, other_rows, other_bfeat, before, acc, feat, rows, bfeat
):
    core = lax.axis_index("core")
    for slot, ref in enumerate((core_ref, far_ref)):
        above = (1 - core) if slot == 0 else core
        x_at = (above * (BX + 1) - 1 - BX // 2).astype(F32)
        for layer in range(2):
            highs, lows, norm, strain = positions(
                ref, layer * 4 * BY, BY, 1, BY, x_at, y_in(), other_shift() if layer else 0.0
            )
            put_neighbour(feat, rows, (slot * 2 + layer) * BY, highs, lows, norm, strain)
    round_tiles(feat, bfeat, 4 * BY, 6)
    acc[...] = before[...]

    def side(slot, carry):
        above = jnp.where(slot == 0, 1 - core, core)
        for y in range(BY):
            a = above * (BX - 1) * BY + y
            pairs = [
                ((slot * 2 + layer) * BY + y + dy - 1, flag_row(a, layer, above * 2, dy))
                for layer in range(2)
                for dy in range(3)
                if 0 <= y + dy - 1 < BY
            ]
            for c, s in enumerate(pair_sums(bcent[a], pairs, bfeat, rows, flags)):
                acc[pl.ds(a * 2 + c, 1), :] += s
        return carry

    lax.fori_loop(0, 2, side, 0, unroll=2)
    middles(1, 2, BX - 1, True, 3, bcent, other_bfeat, other_rows, flags, acc)


def y_kernel(near_ref, far_ref, bcent, flags, own_ref, before, avg_ref, top_ref, feat, rows, bfeat, acc):
    xlo = lax.axis_index("xlo")
    acc[...] = before[...]
    x_in = lax.broadcasted_iota(jnp.int32, (WX, PTS), 0).astype(F32) - (WX // 2)
    for slot, ref in enumerate((near_ref, far_ref)):
        above = (1 - xlo) if slot == 0 else xlo
        y_at = (above * (BY + 1) - 1 - BY // 2).astype(F32)
        for layer in range(2):
            highs, lows, norm, strain = positions(
                ref, layer * 4 * WX, WX, 1, WX, x_in, y_at, other_shift() if layer else 0.0
            )
            put_neighbour(feat, rows, (slot * 2 + layer) * WX, highs, lows, norm, strain)
    round_tiles(feat, bfeat, 4 * WX, 8)

    def side(slot, carry):
        above = jnp.where(slot == 0, 1 - xlo, xlo)
        for x in range(BX):
            a = above * (BY - 1) + x * BY
            pairs = [
                ((slot * 2 + layer) * WX + x + dx, flag_row(a, layer, dx, above * 2))
                for layer in range(2)
                for dx in range(3)
            ]
            for c, s in enumerate(pair_sums(bcent[a], pairs, bfeat, rows, flags)):
                acc[pl.ds(a * 2 + c, 1), :] += s
        return carry

    lax.fori_loop(0, 2, side, 0, unroll=2)
    top = None
    for r in range(0, NB, 12):
        s = [acc[pl.ds(r * 2 + k, 12, stride=2), :] for k in range(2)]
        live = jnp.where(own_ref[pl.ds(3 * NB + r, 12), :] > 0.0, 1.0, 0.0)
        averaged = live * s[0] / (s[1] + 1.0 - live)
        avg_ref[pl.ds(r, 12), :] = averaged
        top = averaged if top is None else jnp.maximum(top, averaged)
    top_ref[...] = jnp.broadcast_to(jnp.max(top, axis=0, keepdims=True), (8, PTS))


def pack_kernel(counts_hbm, coords_hbm, strain_hbm, own_ref, counts_ref, coords_ref, strain_ref, sems):
    copies = [
        pltpu.make_async_copy(source, target, sems.at[n])
        for n, (source, target) in enumerate(
            ((counts_hbm, counts_ref), (strain_hbm, strain_ref), (coords_hbm, coords_ref))
        )
    ]
    for copy in copies:
        copy.start()
    for copy in copies:
        copy.wait()
    slots = lax.broadcasted_iota(jnp.int32, (1, PTS), 1)
    for c in range(3):
        own_ref[pl.ds(c * NB, NB), :] = coords_ref[pl.ds(c * NB, NB), 0, :]
    for b in range(NB):
        live = slots < counts_ref[b // BY, 0, b % BY]
        own_ref[pl.ds(3 * NB + b, 1), :] = jnp.where(live, strain_ref[b], 0.0)


def strips_kernel(own_ref, other_ref, core_ref, far_ref):
    core = lax.axis_index("core")
    for slot, out in enumerate((core_ref, far_ref)):
        above = (1 - core) if slot == 0 else core
        for layer, ref in enumerate((own_ref, other_ref)):
            for c in range(4):
                out[pl.ds((layer * 4 + c) * BY, BY), :] = ref[pl.ds(c * NB + above * (BX - 1) * BY, BY), :]


def columns_kernel(own_ref, other_ref, core_ref, far_ref, near_out, far_out):
    core, xlo = lax.axis_index("core"), lax.axis_index("xlo")
    for slot, out in enumerate((near_out, far_out)):
        y = ((1 - xlo) if slot == 0 else xlo) * (BY - 1)
        for layer, ref in enumerate((own_ref, other_ref)):
            for c in range(4):
                row, halo = (layer * 4 + c) * WX, (layer * 4 + c) * BY
                out[pl.ds(row + 1, BX), :] = ref[pl.ds(c * NB + y, BX, stride=BY), :]
                out[pl.ds(row + (1 - core) * (WX - 1), 1), :] = core_ref[pl.ds(halo + y, 1), :]
                out[pl.ds(row + core * (WX - 1), 1), :] = far_ref[pl.ds(halo + y, 1), :]


def final_kernel(top_ref, avg_ref, old_ref, own_ref, new_ref, damage_ref):
    highest = jnp.max(top_ref[...], keepdims=True) + 1e-06
    for b in range(0, NB, 12):
        averaged = avg_ref[pl.ds(b, 12), :]
        live = jnp.where(own_ref[pl.ds(3 * NB + b, 12), :] > 0.0, 1.0, 0.0)
        new = jnp.maximum(old_ref[pl.ds(b, 12), 0, :], 4.0 * averaged / highest)
        new_ref[pl.ds(b, 12), 0, :] = new
        damage_ref[pl.ds(b, 12), 0, :] = live * (1.0 - jnp.exp(-(new - 1.0) / 2.5) / new)


def call(kernel, outs, ins, scratch=(), us=1, space=VMEM, extra=()):
    return pl.pallas_call(
        kernel,
        out_shape=tuple(jax.ShapeDtypeStruct(s, d) for s, d in outs),
        in_specs=[space] * ins,
        out_specs=tuple(VMEM for _ in outs),
        scratch_shapes=[pltpu.VMEM(s, d) for s, d in scratch] + list(extra),
        compiler_params=pltpu.CompilerParams(vmem_limit_bytes=16 << 20),
        cost_estimate=pl.CostEstimate(flops=us * 400_000_000, bytes_accessed=1 << 16, transcendentals=0),
    )


def feature_scratch(count):
    return [((count * K, PTS), F32), ((count, PTS), F32), ((count, K, PTS), BF16)]


SUMS = ((2 * NB, PTS), F32)


def on_device(coords, strain, kappa_old, counts, pair_mask):
    raw = (counts.reshape(BX, 1, BY), coords.reshape(3 * NB, 1, PTS), strain.reshape(NB, 1, PTS))
    (own,) = call(
        pack_kernel,
        [((4 * NB, PTS), F32)],
        3,
        space=pl.BlockSpec(memory_space=pltpu.HBM),
        extra=[
            pltpu.SMEM((BX, 1, BY), jnp.int32),
            pltpu.VMEM((3 * NB, 1, PTS), F32),
            pltpu.VMEM((NB, 1, PTS), F32),
            pltpu.SemaphoreType.DMA((3,)),
        ],
    )(*(pltpu.with_memory_space_constraint(v, pltpu.HBM) for v in raw))
    swap = [(0, 1), (1, 0)]
    beside = lambda n: [p for i in range(1, n - 1, 2) for p in ((i, i + 1), (i + 1, i))]
    other = lax.ppermute(own, "ply", swap)
    tile = feature_scratch(NB)
    acc, bcent, flags = call(
        own_kernel,
        [SUMS, ((NB, PTS, K), BF16), ((NB * FLAGS, PTS), F32)],
        2,
        [((PTS, PTS), F32), ((NB * K, PTS), F32)] + tile,
        6,
    )(pair_mask.reshape(NB, 1, 26), own)

    strip = ((8 * BY, PTS), F32)
    core, far = call(strips_kernel, [strip, strip], 2)(own, other)
    far = lax.ppermute(far, ("y", "core"), beside(8))
    core = lax.ppermute(core, "core", swap)
    acc, rows, bfeat = call(other_kernel, [SUMS] + tile[1:], 4, tile[:1], 3)(other, bcent, flags, acc)

    column = ((8 * WX, PTS), F32)
    ynear, yfar = call(columns_kernel, [column, column], 4)(own, other, core, far)
    yfar = lax.ppermute(yfar, ("z", "xlo"), beside(16))
    ynear = lax.ppermute(ynear, "xlo", swap)
    (acc,) = call(x_kernel, [SUMS], 7, feature_scratch(4 * BY), 4)(core, far, bcent, flags, rows, bfeat, acc)
    averaged, top = call(y_kernel, [((NB, PTS), F32), ((8, PTS), F32)], 6, feature_scratch(4 * WX) + [SUMS], 2)(
        ynear, yfar, bcent, flags, own, acc
    )

    tops = lax.all_to_all(jnp.broadcast_to(top[:1], (256, PTS)), AXES, 0, 0, tiled=True)
    new, damage = call(final_kernel, [((NB, 1, PTS), F32)] * 2, 4)(tops, averaged, kappa_old.reshape(NB, 1, PTS), own)
    return (new.reshape(1, BX, BY, PTS), damage.reshape(1, BX, BY, PTS))


def solution(mesh):
    fine = Mesh(mesh.devices.reshape(2, 4, 2, 8, 2), AXES)
    gx, gy = ("y", "core"), ("z", "xlo")
    placed = (
        P(None, "ply", gx, gy, None),
        P("ply", gx, gy, None),
        P("ply", gx, gy, None),
        P("ply", gx, gy),
        P("ply", gx, gy, None),
    )

    return jax.shard_map(
        on_device,
        mesh=fine,
        in_specs=placed,
        out_specs=(P("ply", gx, gy, None), P("ply", gx, gy, None)),
        check_vma=False,
    )
```

```python
import jax
import jax.numpy as jnp
from jax import lax
from jax.experimental import pallas as pl
from jax.experimental.pallas import tpu as pltpu
from jax.sharding import Mesh
from jax.sharding import PartitionSpec as P

BX = 6
BY = 6
NB = BX * BY
WX = BX + 2
PTS = 128
K = 16
FLAGS = 32
AXES = ("ply", "y", "core", "z", "xlo")
F32 = jnp.float32
BF16 = jnp.bfloat16
VMEM = pl.BlockSpec(memory_space=pltpu.VMEM)


def pieces_of(v, count):
    out = []
    for _ in range(count):
        high = v.astype(BF16).astype(F32)
        out.append(high)
        v = v - high
    return out


def positions(ref, row, count, stride, step, x_at, y_at, z_at):
    load = lambda c: ref[pl.ds(row + c * step, count, stride=stride), :]
    shifts = (z_at - 0.5, x_at, y_at)
    pieces = [pieces_of(load(c) + shifts[c], 2) for c in range(3)]
    norm = None
    for high, low in pieces:
        p = high + low
        norm = p * p if norm is None else norm + p * p
    return [p[0] for p in pieces], [p[1] for p in pieces], norm, load(3)


def put_neighbour(feat, rows, base, highs, lows, norm, strain):
    count = strain.shape[0]
    one = jnp.ones_like(strain)
    live = jnp.where(strain > 0.0, 1.0, -256.0)
    listed = highs + lows + highs + pieces_of(live - norm, 3) + [one] * 3 + [jnp.zeros_like(strain)]
    for k, v in enumerate(listed):
        feat[pl.ds(base * K + k, count, stride=K), :] = v
    rows[pl.ds(base, count), :] = strain


def put_center(cent, base, highs, lows, norm):
    count = norm.shape[0]
    one = jnp.ones_like(norm)
    twice = [2.0 * v for v in highs]
    listed = twice + twice + [2.0 * v for v in lows] + [one] * 3 + pieces_of(-norm, 3) + [jnp.zeros_like(norm)]
    for k, v in enumerate(listed):
        cent[pl.ds(base * K + k, count, stride=K), :] = v


def round_tiles(feat, bfeat, count, unroll):
    def one(b, carry):
        bfeat[b] = feat[pl.ds(pl.multiple_of(b * K, K), K), :].astype(BF16)
        return carry

    lax.fori_loop(0, count, one, 0, unroll=unroll)


def pair_sums(center, pairs, bfeat, rows, mask):
    spot = jnp.where(lax.broadcasted_iota(jnp.int32, (K, PTS), 0) == 9, 1.0, 0.0)
    sums = [[None] * 16, [None] * 16]
    for t in range(0, len(pairs), 2):
        some = pairs[t : t + 2]
        tiles = []
        for b, flag in some:
            tile = bfeat[b]
            if flag is not None:
                tile = tile + (spot * jnp.broadcast_to(mask[pl.ds(flag, 1), :], (K, PTS))).astype(BF16)
            tiles.append(tile)
        rhs = jnp.concatenate(tiles, axis=1) if len(tiles) > 1 else tiles[0]
        gap = jnp.dot(center, rhs, preferred_element_type=F32)
        for n, (b, flag) in enumerate(some):
            strain = jnp.broadcast_to(rows[pl.ds(b, 1), :], (8, PTS))
            for r in range(16):
                w = jnp.maximum(gap[r * 8 : r * 8 + 8, n * PTS : (n + 1) * PTS], 0.0)
                w = w * w
                v = w * strain
                sums[0][r] = v if sums[0][r] is None else sums[0][r] + v
                sums[1][r] = w if sums[1][r] is None else sums[1][r] + w
    return [jnp.sum(jnp.concatenate(s, axis=0).T, axis=0, keepdims=True) for s in sums]


def y_in():
    return lax.broadcasted_iota(jnp.int32, (BY, PTS), 0).astype(F32) - (BY // 2)


def flag_row(a, layer, dx, dy):
    t = dx * 3 + dy
    if layer:
        return a * FLAGS + t + jnp.where(lax.axis_index("ply") == 0, 17, 0)
    return a * FLAGS + jnp.where(t == 4, FLAGS - 1, 9 + t - jnp.where(t > 4, 1, 0))


def fill_flags(mask_ref, turned, flags):
    turned[...] = jnp.zeros_like(turned)
    turned[0:NB, 0:26] = (mask_ref[:, 0, :] * 256 - 256).astype(F32)
    across = turned[...].T
    for a in range(NB):
        flags[a * FLAGS : (a + 1) * FLAGS, :] = jnp.broadcast_to(across[0:FLAGS, a : a + 1], (FLAGS, PTS))


def strip_sums(layer, x, first, dxs, bcent, bfeat, rows, flags, acc, add):
    for y in range(BY):
        a = x * BY + y
        pairs = []
        for n in range(dxs):
            for dy in range(3):
                if 0 <= y + dy - 1 < BY:
                    at_self = layer == 0 and dy == 1 and dxs == 3 and n == 1
                    flag = None if at_self else flag_row(a, layer, first + n - x + 1, dy)
                    pairs.append(((first + n) * BY + y + dy - 1, flag))
        for c, s in enumerate(pair_sums(bcent[a], pairs, bfeat, rows, flags)):
            if add:
                s = s + acc[pl.ds(a * 2 + c, 1), :]
            acc[pl.ds(a * 2 + c, 1), :] = s


def edges(layer, add, *refs):
    def edge(e, carry):
        strip_sums(layer, e * (BX - 1), e * (BX - 2), 2, *refs, add)
        return carry

    lax.fori_loop(0, 2, edge, 0, unroll=2)


def middles(layer, low, high, add, unroll, *refs):
    def middle(x, carry):
        strip_sums(layer, x, x - 1, 3, *refs, add)
        return carry

    lax.fori_loop(low, high, middle, 0, unroll=unroll)


def other_shift():
    return (1 - 2 * lax.axis_index("ply")).astype(F32)


def own_kernel(mask_ref, own_ref, acc, bcent, flags, turned, cent, feat, rows, bfeat):
    fill_flags(mask_ref, turned, flags)
    for x in range(BX):
        highs, lows, norm, strain = positions(own_ref, x * BY, BY, 1, NB, float(x - BX // 2), y_in(), 0.0)
        put_neighbour(feat, rows, x * BY, highs, lows, norm, strain)
        put_center(cent, x * BY, highs, lows, norm)
    round_tiles(feat, bfeat, NB, 12)

    def turn(a, carry):
        bcent[a] = cent[pl.ds(pl.multiple_of(a * K, K), K), :].T.astype(BF16)
        return carry

    lax.fori_loop(0, NB, turn, 0, unroll=NB)
    refs = (bcent, bfeat, rows, flags, acc)
    edges(0, False, *refs)
    middles(0, 1, BX - 1, False, 4, *refs)


def other_kernel(other_ref, bcent, flags, before, acc, rows, bfeat, feat):
    for x in range(BX):
        highs, lows, norm, strain = positions(other_ref, x * BY, BY, 1, NB, float(x - BX // 2), y_in(), other_shift())
        put_neighbour(feat, rows, x * BY, highs, lows, norm, strain)
    round_tiles(feat, bfeat, NB, 12)
    acc[...] = before[...]
    refs = (bcent, bfeat, rows, flags, acc)
    edges(1, True, *refs)
    middles(1, 1, 3, True, 2, *refs)


def x_kernel(
    core_ref, far_ref, bcent, flags, other_rows, other_bfeat, before, acc, feat, rows, bfeat
):
    core = lax.axis_index("core")
    for slot, ref in enumerate((core_ref, far_ref)):
        above = (1 - core) if slot == 0 else core
        x_at = (above * (BX + 1) - 1 - BX // 2).astype(F32)
        for layer in range(2):
            highs, lows, norm, strain = positions(
                ref, layer * 4 * BY, BY, 1, BY, x_at, y_in(), other_shift() if layer else 0.0
            )
            put_neighbour(feat, rows, (slot * 2 + layer) * BY, highs, lows, norm, strain)
    round_tiles(feat, bfeat, 4 * BY, 6)
    acc[...] = before[...]

    def side(slot, carry):
        above = jnp.where(slot == 0, 1 - core, core)
        for y in range(BY):
            a = above * (BX - 1) * BY + y
            pairs = [
                ((slot * 2 + layer) * BY + y + dy - 1, flag_row(a, layer, above * 2, dy))
                for layer in range(2)
                for dy in range(3)
                if 0 <= y + dy - 1 < BY
            ]
            for c, s in enumerate(pair_sums(bcent[a], pairs, bfeat, rows, flags)):
                acc[pl.ds(a * 2 + c, 1), :] += s
        return carry

    lax.fori_loop(0, 2, side, 0, unroll=2)
    middles(1, 3, BX - 1, True, 2, bcent, other_bfeat, other_rows, flags, acc)


def y_kernel(near_ref, far_ref, bcent, flags, own_ref, before, avg_ref, top_ref, feat, rows, bfeat, acc):
    xlo = lax.axis_index("xlo")
    acc[...] = before[...]
    x_in = lax.broadcasted_iota(jnp.int32, (WX, PTS), 0).astype(F32) - (WX // 2)
    for slot, ref in enumerate((near_ref, far_ref)):
        above = (1 - xlo) if slot == 0 else xlo
        y_at = (above * (BY + 1) - 1 - BY // 2).astype(F32)
        for layer in range(2):
            highs, lows, norm, strain = positions(
                ref, layer * 4 * WX, WX, 1, WX, x_in, y_at, other_shift() if layer else 0.0
            )
            put_neighbour(feat, rows, (slot * 2 + layer) * WX, highs, lows, norm, strain)
    round_tiles(feat, bfeat, 4 * WX, 8)

    def side(slot, carry):
        above = jnp.where(slot == 0, 1 - xlo, xlo)
        for x in range(BX):
            a = above * (BY - 1) + x * BY
            pairs = [
                ((slot * 2 + layer) * WX + x + dx, flag_row(a, layer, dx, above * 2))
                for layer in range(2)
                for dx in range(3)
            ]
            for c, s in enumerate(pair_sums(bcent[a], pairs, bfeat, rows, flags)):
                acc[pl.ds(a * 2 + c, 1), :] += s
        return carry

    lax.fori_loop(0, 2, side, 0, unroll=2)
    top = None
    for r in range(0, NB, 12):
        s = [acc[pl.ds(r * 2 + k, 12, stride=2), :] for k in range(2)]
        live = jnp.where(own_ref[pl.ds(3 * NB + r, 12), :] > 0.0, 1.0, 0.0)
        averaged = live * s[0] / (s[1] + 1.0 - live)
        avg_ref[pl.ds(r, 12), :] = averaged
        top = averaged if top is None else jnp.maximum(top, averaged)
    top_ref[...] = jnp.broadcast_to(jnp.max(top, axis=0, keepdims=True), (8, PTS))


def pack_kernel(counts_hbm, coords_hbm, strain_hbm, own_ref, counts_ref, coords_ref, strain_ref, sems):
    copies = [
        pltpu.make_async_copy(source, target, sems.at[n])
        for n, (source, target) in enumerate(
            ((counts_hbm, counts_ref), (strain_hbm, strain_ref), (coords_hbm, coords_ref))
        )
    ]
    for copy in copies:
        copy.start()
    for copy in copies:
        copy.wait()
    slots = lax.broadcasted_iota(jnp.int32, (1, PTS), 1)
    for c in range(3):
        own_ref[pl.ds(c * NB, NB), :] = coords_ref[pl.ds(c * NB, NB), 0, :]
    for b in range(NB):
        live = slots < counts_ref[b // BY, 0, b % BY]
        own_ref[pl.ds(3 * NB + b, 1), :] = jnp.where(live, strain_ref[b], 0.0)


def strips_kernel(own_ref, other_ref, core_ref, far_ref):
    core = lax.axis_index("core")
    for slot, out in enumerate((core_ref, far_ref)):
        above = (1 - core) if slot == 0 else core
        for layer, ref in enumerate((own_ref, other_ref)):
            for c in range(4):
                out[pl.ds((layer * 4 + c) * BY, BY), :] = ref[pl.ds(c * NB + above * (BX - 1) * BY, BY), :]


def columns_kernel(own_ref, other_ref, core_ref, far_ref, near_out, far_out):
    core, xlo = lax.axis_index("core"), lax.axis_index("xlo")
    for slot, out in enumerate((near_out, far_out)):
        y = ((1 - xlo) if slot == 0 else xlo) * (BY - 1)
        for layer, ref in enumerate((own_ref, other_ref)):
            for c in range(4):
                row, halo = (layer * 4 + c) * WX, (layer * 4 + c) * BY
                out[pl.ds(row + 1, BX), :] = ref[pl.ds(c * NB + y, BX, stride=BY), :]
                out[pl.ds(row + (1 - core) * (WX - 1), 1), :] = core_ref[pl.ds(halo + y, 1), :]
                out[pl.ds(row + core * (WX - 1), 1), :] = far_ref[pl.ds(halo + y, 1), :]


def final_kernel(top_ref, avg_ref, old_ref, own_ref, new_ref, damage_ref):
    highest = jnp.max(top_ref[...], keepdims=True) + 1e-06
    for b in range(0, NB, 12):
        averaged = avg_ref[pl.ds(b, 12), :]
        live = jnp.where(own_ref[pl.ds(3 * NB + b, 12), :] > 0.0, 1.0, 0.0)
        new = jnp.maximum(old_ref[pl.ds(b, 12), 0, :], 4.0 * averaged / highest)
        new_ref[pl.ds(b, 12), 0, :] = new
        damage_ref[pl.ds(b, 12), 0, :] = live * (1.0 - jnp.exp(-(new - 1.0) / 2.5) / new)


def call(kernel, outs, ins, scratch=(), us=1, space=VMEM, extra=()):
    return pl.pallas_call(
        kernel,
        out_shape=tuple(jax.ShapeDtypeStruct(s, d) for s, d in outs),
        in_specs=[space] * ins,
        out_specs=tuple(VMEM for _ in outs),
        scratch_shapes=[pltpu.VMEM(s, d) for s, d in scratch] + list(extra),
        compiler_params=pltpu.CompilerParams(vmem_limit_bytes=16 << 20),
        cost_estimate=pl.CostEstimate(flops=us * 400_000_000, bytes_accessed=1 << 16, transcendentals=0),
    )


def feature_scratch(count):
    return [((count * K, PTS), F32), ((count, PTS), F32), ((count, K, PTS), BF16)]


SUMS = ((2 * NB, PTS), F32)


def on_device(coords, strain, kappa_old, counts, pair_mask):
    raw = (counts.reshape(BX, 1, BY), coords.reshape(3 * NB, 1, PTS), strain.reshape(NB, 1, PTS))
    (own,) = call(
        pack_kernel,
        [((4 * NB, PTS), F32)],
        3,
        space=pl.BlockSpec(memory_space=pltpu.HBM),
        extra=[
            pltpu.SMEM((BX, 1, BY), jnp.int32),
            pltpu.VMEM((3 * NB, 1, PTS), F32),
            pltpu.VMEM((NB, 1, PTS), F32),
            pltpu.SemaphoreType.DMA((3,)),
        ],
    )(*(pltpu.with_memory_space_constraint(v, pltpu.HBM) for v in raw))
    swap = [(0, 1), (1, 0)]
    beside = lambda n: [p for i in range(1, n - 1, 2) for p in ((i, i + 1), (i + 1, i))]
    other = lax.ppermute(own, "ply", swap)
    tile = feature_scratch(NB)
    acc, bcent, flags = call(
        own_kernel,
        [SUMS, ((NB, PTS, K), BF16), ((NB * FLAGS, PTS), F32)],
        2,
        [((PTS, PTS), F32), ((NB * K, PTS), F32)] + tile,
        6,
    )(pair_mask.reshape(NB, 1, 26), own)

    strip = ((8 * BY, PTS), F32)
    core, far = call(strips_kernel, [strip, strip], 2)(own, other)
    far = lax.ppermute(far, ("y", "core"), beside(8))
    core = lax.ppermute(core, "core", swap)
    acc, rows, bfeat = call(other_kernel, [SUMS] + tile[1:], 4, tile[:1], 3)(other, bcent, flags, acc)

    column = ((8 * WX, PTS), F32)
    ynear, yfar = call(columns_kernel, [column, column], 4)(own, other, core, far)
    yfar = lax.ppermute(yfar, ("z", "xlo"), beside(16))
    ynear = lax.ppermute(ynear, "xlo", swap)
    (acc,) = call(x_kernel, [SUMS], 7, feature_scratch(4 * BY), 4)(core, far, bcent, flags, rows, bfeat, acc)
    averaged, top = call(y_kernel, [((NB, PTS), F32), ((8, PTS), F32)], 6, feature_scratch(4 * WX) + [SUMS], 2)(
        ynear, yfar, bcent, flags, own, acc
    )

    tops = lax.all_to_all(jnp.broadcast_to(top[:1], (256, PTS)), AXES, 0, 0, tiled=True)
    new, damage = call(final_kernel, [((NB, 1, PTS), F32)] * 2, 4)(tops, averaged, kappa_old.reshape(NB, 1, PTS), own)
    return (new.reshape(1, BX, BY, PTS), damage.reshape(1, BX, BY, PTS))


def solution(mesh):
    fine = Mesh(mesh.devices.reshape(2, 4, 2, 8, 2), AXES)
    gx, gy = ("y", "core"), ("z", "xlo")
    placed = (
        P(None, "ply", gx, gy, None),
        P("ply", gx, gy, None),
        P("ply", gx, gy, None),
        P("ply", gx, gy),
        P("ply", gx, gy, None),
    )

    return jax.shard_map(
        on_device,
        mesh=fine,
        in_specs=placed,
        out_specs=(P("ply", gx, gy, None), P("ply", gx, gy, None)),
        check_vma=False,
    )
```
